32 devices in a mesh: seq: 8 (over z, x), head: 4 (over y, core).
Axes of the slice: x: 2, y: 2, z: 4, core: 2. Of those that a mesh axis runs over, the one named last changes fastest.
Arguments:
- signal: bfloat16 [4096, 128, 64], P('seq', 'head'), may hold values from -6 to 6
- step_raw: bfloat16 [4096, 128], P('seq', 'head'), may hold values from -3 to 3
- key_proj: bfloat16 [4096, 128], P('seq'), may hold values from -0.69921875 to 0.69921875
- query_proj: bfloat16 [4096, 128], P('seq'), may hold values from -0.69921875 to 0.69921875
- decay_log: float32 [128], P('head'), may hold values from -9 to -3
- skip_gain: float32 [128], P('head'), may hold values from 0.5 to 1.5
- lengths: int32 [6], replicated, may hold values from 1 to 2048, 4096 in all
- cotangent: bfloat16 [4096, 128, 64], P('seq', 'head'), may hold values from -0.59765625 to 0.59765625
Outputs:
- output: bfloat16 [4096, 128, 64], P('seq', 'head')
- grad_signal: bfloat16 [4096, 128, 64], P('seq', 'head')
- grad_keys: bfloat16 [4096, 128], P('seq')
- grad_queries: bfloat16 [4096, 128], P('seq')
The draws below stay inside these ranges and needn't reach their ends.
Inputs may be any that keep to these rules, and one draw needn't show every extreme that they name: The 6 lengths sum to 4096; the longest is exactly 2048.
All inputs are finite; a program needn't handle non-finite values.
Results may differ from the reference program's by a relative error of at most 0.001.
Values may be sent and summed in bfloat16 or wider, within the bound.
A program may use at most 128 MiB of HBM per device.

```python
import math
import jax
import jax.numpy as jnp
import numpy as np
from jax import lax

H = 128
P_SIZE = 64
N = 128
SPAN = 256
DOCS = 6
TOKENS = 4096


def levels(key, shape, split, low, top_value):
    loudness = 1.0
    for position, shards_of in split:
        steps = jax.random.uniform(jax.random.fold_in(jax.random.fold_in(key, 6), position), (shards_of,), jnp.float32, low / len(split), top_value / len(split))
        loudness = loudness * jnp.repeat(jnp.exp(steps), shape[position] // shards_of).reshape((-1,) + (1,) * (len(shape) - 1 - position))
    return loudness


def split_up(amount, total, bound, slope):
    loads = [(1 << 20) // math.isqrt(grade ** slope) + 1 for grade in range(2, amount + 1)]
    surplus, holding = total - bound - (amount - 1), [1] * (amount - 1)
    while surplus > 0:
        movable = [i for i in range(amount - 1) if holding[i] < bound]
        whole, remaining = sum([loads[i] for i in movable]), surplus
        for i in movable:
            extra = min(bound - holding[i], max(1, remaining * loads[i] // whole), surplus)
            holding[i] = holding[i] + extra
            surplus = surplus - extra
    return np.array([bound] + holding)


def uneven(rng, number_of, total, most, slope):
    if number_of == 2:
        one = jax.random.randint(rng, (), max(1, total - most), min(most, total - 1) + 1)
        return jnp.stack([one, total - one])
    sizes = jnp.asarray(split_up(number_of, total, most, slope), jnp.int32)
    pairs = (number_of - 1) // 2
    source_of, receiver = sizes[1:1 + 2 * pairs:2], sizes[2:2 + 2 * pairs:2]
    slack = jnp.minimum(source_of - 1, most - receiver)
    moved = jax.random.randint(jax.random.fold_in(rng, 1), (pairs,), 0, 1 << 20) % (slack + 1)
    sizes = sizes.at[1:1 + 2 * pairs:2].set(source_of - moved).at[2:2 + 2 * pairs:2].set(receiver + moved)
    return sizes[jax.random.permutation(jax.random.fold_in(rng, 2), number_of)]


def centred(stream_key, dims, spread, limit, cuts=(), kind=jnp.bfloat16):
    entries = spread * jax.random.normal(stream_key, dims, jnp.float32)
    if cuts:
        entries = entries * levels(stream_key, dims, cuts, -0.22, 0.18)
    return jnp.clip(entries, -limit, limit).astype(kind)


def setup_inputs(seed: int = 0) -> dict:
    seeds = jax.random.split(jax.random.key(seed), 9)
    return {
        "signal": centred(seeds[0], (TOKENS, H, P_SIZE), 1.0, 6.0, ((0, 8), (1, 4))),
        "step_raw": centred(seeds[1], (TOKENS, H), 1.0, 3.0, ((0, 8), (1, 4))),
        "key_proj": centred(seeds[2], (TOKENS, N), 0.12, 0.69921875, ((0, 8),)),
        "query_proj": centred(seeds[3], (TOKENS, N), 0.12, 0.69921875, ((0, 8),)),
        "decay_log": jnp.clip(-9.0 + 6.0 * jax.random.uniform(seeds[4], (H,), jnp.float32) ** levels(seeds[4], (H,), ((0, 4),), -0.2, 0.2), -9.0, -3.0),
        "skip_gain": jnp.clip(0.5 + 1.0 * jax.random.uniform(seeds[5], (H,), jnp.float32) ** levels(seeds[5], (H,), ((0, 4),), -0.2, 0.2), 0.5, 1.5),
        "lengths": uneven(seeds[6], DOCS, TOKENS, TOKENS // 2, 2).astype(jnp.int32),
        "cotangent": centred(seeds[7], (TOKENS, H, P_SIZE), 0.1, 0.59765625, ((0, 8), (1, 4))),
    }


highest = lax.Precision.HIGHEST

def span_pass(drive, keys_in, queries_in, logdec, segment, prior_seg, init_state):
    length_all, heads_held, lanes_held = drive.shape
    state_width = keys_in.shape[1]
    blocks_count = length_all // SPAN
    seg_blocks = segment.reshape(blocks_count, SPAN)
    previous = jnp.concatenate([jnp.reshape(prior_seg, (1,)).astype(jnp.int32), seg_blocks[:-1, -1]]).astype(jnp.int32)
    offsets = jnp.arange(SPAN, dtype=jnp.int32)
    causal = offsets[:, None] >= offsets[None, :]

    def advance(carry_state, pieces):
        drive_block, keys_block, queries_block, decay_block, seg_block, previous_seg = pieces
        local_cum = jnp.cumsum(decay_block, axis=0)
        same_doc = ((seg_block[:, None] == seg_block[None, :]) & causal)[:, :, None]
        log_gap = jnp.where(same_doc, local_cum[:, None, :] - local_cum[None, :, :], 0.0)
        weight = jnp.where(same_doc, jnp.exp(log_gap), 0.0)
        gram_block = jnp.dot(queries_block, keys_block.T, precision=highest)
        within = jnp.einsum('tsh,shp->thp', weight * gram_block[:, :, None], drive_block, precision=highest)
        entering = jnp.where((seg_block == previous_seg)[:, None], jnp.exp(local_cum), 0.0)
        carried = jnp.einsum('tn,hpn->thp', queries_block, carry_state, precision=highest) * entering[:, :, None]
        to_end = jnp.where((seg_block == seg_block[-1])[:, None], jnp.exp(local_cum[-1][None, :] - local_cum), 0.0)
        fresh_state = jnp.einsum('sh,sn,shp->hpn', to_end, keys_block, drive_block, precision=highest)
        surviving = jnp.where(seg_block[-1] == previous_seg, jnp.exp(local_cum[-1]), 0.0)
        new_state = carry_state * surviving[:, None, None] + fresh_state
        return (new_state, within + carried)
    stacked = (drive.reshape(blocks_count, SPAN, heads_held, lanes_held), keys_in.reshape(blocks_count, SPAN, state_width), queries_in.reshape(blocks_count, SPAN, state_width), logdec.reshape(blocks_count, SPAN, heads_held), seg_blocks, previous)
    last_state, scanned = lax.scan(jax.checkpoint(advance), init_state, stacked)
    return (scanned.reshape(length_all, heads_held, lanes_held), last_state)

def reference(signal, step_raw, key_proj, query_proj, decay_log, skip_gain, lengths, cotangent):
    all_tokens, heads_all, width_p = signal.shape
    state_width = key_proj.shape[1]
    stepsize = jax.nn.softplus(step_raw.astype(jnp.float32))
    decay_rate = -jnp.exp(decay_log)
    logdec = stepsize * decay_rate[None, :]
    doc_ends = jnp.cumsum(lengths).astype(jnp.int32)
    places = jnp.arange(all_tokens, dtype=jnp.int32)
    segment = lax.optimization_barrier(jnp.sum((places[:, None] >= doc_ends[None, :]).astype(jnp.int32), axis=1)).astype(jnp.int32)
    signal_f = signal.astype(jnp.float32)
    cotan_f = cotangent.astype(jnp.float32)
    drive = stepsize[:, :, None] * signal_f
    zero_state = jnp.zeros((heads_all, width_p, state_width), jnp.float32)
    prior = jnp.full((), -1, jnp.int32)

    def forward(drive_in, keys_in, queries_in):
        return span_pass(drive_in, keys_in, queries_in, logdec, segment, prior, zero_state)[0]
    scanned, pullback = jax.vjp(forward, drive, key_proj.astype(jnp.float32), query_proj.astype(jnp.float32))
    grad_drive, grad_keys, grad_queries = pullback(cotan_f)
    output = (scanned + skip_gain[None, :, None] * signal_f).astype(jnp.bfloat16)
    grad_signal = (grad_drive * stepsize[:, :, None] + skip_gain[None, :, None] * cotan_f).astype(jnp.bfloat16)
    return (output, grad_signal, grad_keys.astype(jnp.bfloat16), grad_queries.astype(jnp.bfloat16))
```

```python
import functools

import jax
import jax.numpy as jnp
from jax import lax
from jax.experimental import pallas as pl
from jax.experimental.pallas import tpu as pltpu
from jax.sharding import PartitionSpec as P

MESH = pl.DeviceIdType.MESH
F32 = jnp.float32
BF16 = jnp.bfloat16
GROUP = 4


def mm(a, b, ca=1, cb=0):
    return lax.dot_general(a, b, (((ca,), (cb,)), ((), ())), preferred_element_type=F32)


def split(a):
    hi = a.astype(BF16)
    return hi, (a - hi.astype(F32)).astype(BF16)


def mm3(a, b, ca=1, cb=0):
    return mm(a[0], b[0], ca, cb) + mm(a[0], b[1], ca, cb) + mm(a[1], b[0], ca, cb)


def put(ref, w, k, v):
    hb, width, state = v.shape
    top = jnp.max(jnp.abs(v), axis=1)
    power = jnp.ceil(jnp.log2(jnp.maximum(top, 1e-30)))
    code = jnp.round(v * (jnp.exp2(-power) * 32000.0)[:, None, :])
    ref[w, k, : hb * width] = code.reshape(hb * width, state).astype(jnp.int32).astype(jnp.int16)
    pad = jnp.concatenate([power, jnp.zeros((16 - hb, state), F32)], axis=0)
    ref[w, k, hb * width :] = pad.astype(jnp.int32).astype(jnp.int16)


def get(ref, w, k, hb, width, state):
    power = ref[w, k, hb * width :].astype(jnp.int32).astype(F32)[:hb]
    code = ref[w, k, : hb * width].astype(jnp.int32).astype(F32).reshape(hb, width, state)
    return code * (jnp.exp2(power) * (1.0 / 32000.0))[:, None, :]


def kernel(
    nseq, nhead, len_ref, sig, cot, step_ref, key_ref, query_ref, dl_ref, sk_ref,
    res_ref, gk_ref, gq_ref,
    inp, hi, lo, ys, macc, gh, gl, gth, gtl, proj, fac, pas, pasr, scl, skp, loc, ins,
    xq, xr, zq, zr, tq, tr, gacc, gloc, gsc, grc, hx, gfin,
    isem, psem, xsem, zsem, tsem, csem, ysem, fsem,
):
    _, heads, width, tok = inp.shape
    state = key_ref.shape[1]
    blocks = 2 * GROUP
    hb = heads // blocks
    rows = hb * width
    half = tok // 2
    ny = nhead // 2
    me, hd = lax.axis_index("seq"), lax.axis_index("head")
    x, z = lax.rem(me, 2), me // 2
    yy, core = hd // 2, lax.rem(hd, 2)
    nz = nseq // 2
    partner = me + 1 - 2 * x
    mate = hd + 1 - 2 * core
    early = jnp.where(z < nz // 2, 0, 1)
    late = 1 - early

    def can_take(w):
        return jnp.where(w == 0, z, nz - 1 - z) > 0

    def can_send(w):
        return jnp.where(w == 0, nz - 1 - z, z) > 0

    sides = (1 - x, x)

    def in_copy(src, w, j):
        part = pl.ds(sides[j] * (heads // 2), heads // 2)
        return pltpu.make_async_copy(src.at[part], inp.at[w, part], isem.at[w, j])

    for j in range(2):
        in_copy(sig, 0, j).start()
        in_copy(cot, 1, j).start()

    barrier = pltpu.get_barrier_semaphore()

    def greet(seq, head):
        pl.semaphore_signal(barrier, inc=1, device_id=(seq, head), device_id_type=MESH)

    greet(partner, hd)

    @pl.when(z > 0)
    def _():
        greet(me - 2, hd)

    @pl.when(z < nz - 1)
    def _():
        greet(me + 2, hd)

    greet(me, mate)
    for d in range(1, ny):
        greet(me, lax.rem(hd + 2 * d, nhead))

    def hblock(b):
        return pl.ds(b * hb, hb)

    def rcopy(src, dst, sems, index, seq, head=None):
        return pltpu.make_async_remote_copy(
            src_ref=src, dst_ref=dst, send_sem=sems.at[(0,) + index], recv_sem=sems.at[(1,) + index],
            device_id=(seq, hd if head is None else head), device_id_type=MESH,
        )

    def p_copy():
        return rcopy(pas, pasr, psem, (), partner)

    def x_copy(w, k):
        return rcopy(xq.at[w, k], xr.at[w, k], xsem, (w, k), partner)

    def z_copy(w, k):
        return rcopy(zq.at[w, k], zr.at[w, k], zsem, (w, k), me + 2 - 4 * w)

    def t_copy(w, k):
        return rcopy(tq.at[w, k], tr.at[w, k], tsem, (w, k), partner)

    start = me * tok
    end, ends = jnp.int32(0), []
    for k in range(len_ref.shape[0]):
        end = end + len_ref[k]
        ends.append(end)

    def segment(places):
        total = jnp.zeros_like(places)
        for value in ends:
            total = total + jnp.where(places >= value, 1, 0)
        return total

    seg_last = segment(start + tok - 1)
    prior = jnp.where(start > 0, segment(start - 1), -1)
    seg_col = segment(start + lax.broadcasted_iota(jnp.int32, (tok, 1), 0))
    seg_row = segment(start + lax.broadcasted_iota(jnp.int32, (1, tok), 1))
    r_id = lax.broadcasted_iota(jnp.int32, (tok, tok), 0)
    c_id = lax.broadcasted_iota(jnp.int32, (tok, tok), 1)
    upper = jnp.where(r_id <= c_id, 1.0, 0.0).astype(BF16)

    raw = step_ref[...].astype(F32)
    size = jnp.maximum(raw, 0.0) + jnp.log1p(jnp.exp(-jnp.abs(raw)))
    eye = lax.broadcasted_iota(jnp.int32, (heads, heads), 0) == lax.broadcasted_iota(
        jnp.int32, (heads, heads), 1
    )
    column = lambda ref: jnp.sum(jnp.where(eye, ref[...], 0.0), axis=1, keepdims=True)
    logdec = size * (-jnp.exp(column(dl_ref)))
    one = logdec.astype(BF16)
    rest = logdec - one.astype(F32)
    two, three = split(rest)
    cum = mm(three, upper) + mm(two, upper) + mm(one, upper)
    mid, final = cum[:, half - 1 : half], cum[:, tok - 1 : tok]
    e = jnp.exp(cum - mid)
    f = size * jnp.exp(mid - cum)
    lanes = (heads, state)
    passing = jnp.broadcast_to(jnp.where(seg_last == prior, jnp.exp(final), 0.0), lanes)
    to_last = jnp.broadcast_to(jnp.exp(final - mid), lanes)
    to_mid = jnp.broadcast_to(jnp.exp(mid), lanes)
    skips = jnp.broadcast_to(column(sk_ref), lanes)
    for b in range(blocks):
        part = slice(b * hb, (b + 1) * hb)
        fac[0, b], fac[1, b] = f[part], e[part]
        scl[0, b], scl[1, b] = to_last[part], to_mid[part]
        pas[b], skp[b] = passing[part], skips[part]

    keys, queries = key_ref[...], query_ref[...]
    km = jnp.where(seg_col == seg_last, keys.astype(F32), 0.0).astype(BF16)
    qm = jnp.where(seg_col == prior, queries.astype(F32), 0.0).astype(BF16)
    for j in range(2):
        proj[0, :, j * state : (j + 1) * state] = km
        proj[1, :, j * state : (j + 1) * state] = qm

    for w in range(2):
        @pl.when(jnp.logical_not(can_take(w)))
        def _():
            zr[w] = jnp.zeros_like(zr[w])

    pl.semaphore_wait(
        barrier, 1 + ny + jnp.where(z > 0, 1, 0) + jnp.where(z < nz - 1, 1, 0)
    )
    p_copy().start()

    def p1(w, b):
        t = inp[w, hblock(b)].astype(F32) * fac[w, b][:, None, :]
        top, low = split(t.reshape(rows, tok))
        hi[w, b], lo[w, b] = top, low
        pr = proj[w, :, :state]
        return (mm(top, pr) + mm(low, pr)).reshape(hb, width, state) * scl[w, b][:, None, :]

    for w in (early, late):
        in_copy(sig, w, 0).wait()

        @pl.loop(0, GROUP)
        def _(k):
            put(xq, w, k, p1(w, (1 - x) * GROUP + k))
            x_copy(w, k).start()

    for w in (early, late):
        in_copy(sig, w, 1).wait()

        @pl.loop(0, GROUP)
        def _(k):
            b = x * GROUP + k
            loc[w, b] = p1(w, b)

    same = seg_col == seg_row
    gram = jnp.where(same & (r_id >= c_id), mm(queries, keys, 1, 1), 0.0)
    gh[...], gl[...] = split(gram)
    gram_t = jnp.where(same & (r_id <= c_id), mm(keys, queries, 1, 1), 0.0)
    gth[...], gtl[...] = split(gram_t)
    macc[...] = jnp.zeros_like(macc)
    gacc[...] = jnp.zeros_like(gacc)

    def p2(b):
        bb = (hi[0, b], lo[0, b])
        aa = (hi[1, b], lo[1, b])
        b0 = (bb[0][:, :half], bb[1][:, :half])
        a0 = (aa[0][:, :half], aa[1][:, :half])
        a1 = (aa[0][:, half:], aa[1][:, half:])
        ys[0, b, :, :half] = mm3(b0, (gth[:half, :half], gtl[:half, :half]))
        ys[0, b, :, half:] = mm3(bb, (gth[:, half:], gtl[:, half:]))
        ys[1, b, :, half:] = mm3(a1, (gh[half:, half:], gl[half:, half:]))
        ys[1, b, :, :half] = mm3(aa, (gh[:, :half], gl[:, :half]))
        macc[:half, :half] += mm3(a0, b0, 0, 0)
        macc[half:, :] += mm3(a1, bb, 0, 0)

    def handle(w, k):
        b = x * GROUP + k
        first = x == w
        x_copy(w, k).wait_recv()

        @pl.when(can_take(w))
        def _():
            z_copy(w, k).wait_recv()

        own, other = pas[b][:, None, :], pasr[b][:, None, :]
        mine, theirs = loc[w, b], get(xr, w, k, hb, width, state)
        pass0, pass1 = jnp.where(first, own, other), jnp.where(first, other, own)
        loc0, loc1 = jnp.where(first, mine, theirs), jnp.where(first, theirs, mine)
        in0 = get(zr, w, k, hb, width, state)
        in1 = pass0 * in0 + loc0

        @pl.when(can_send(w))
        def _():
            put(zq, w, k, pass1 * in1 + loc1)
            z_copy(w, k).start()

        put(tq, w, k, jnp.where(first, in1, in0))
        t_copy(w, k).start()
        ins[w, b] = jnp.where(first, in0, in1)

    def p3(w, b):
        st = split((ins[w, b] * scl[1 - w, b][:, None, :]).reshape(rows, state))
        both = jnp.concatenate(st, axis=1)
        m = mm(both, hi[1 - w, b], 0, 0)
        gacc[w] += m[:state] + m[state:] + mm(st[0], lo[1 - w, b], 0, 0)
        y = ys[w, b] + mm(both, proj[1 - w], 1, 1)
        skip = skp[b][:, 0:1][:, :, None]
        res_ref[w, hblock(b)] = (
            y.reshape(hb, width, tok) * fac[1 - w, b][:, None, :]
            + skip * inp[w, hblock(b)].astype(F32)
        ).astype(BF16)

    def p3_taken(w, k):
        t_copy(w, k).wait_recv()
        b = (1 - x) * GROUP + k
        ins[w, b] = get(tr, w, k, hb, width, state)
        p3(w, b)

    def c_copy(w):
        return rcopy(gsc.at[w, 1 - core], grc.at[w], csem, (w,), me, mate)

    def y_copy(w, d, slot):
        return rcopy(hx.at[w, slot], hx.at[w, slot], ysem, (w, d), me, lax.rem(hd + 2 * d, nhead))

    def f_copy(w, slot):
        return rcopy(gfin.at[w, slot], gfin.at[w, slot], fsem, (w,), me, mate)

    def reduce_core(w):
        kept = seg_row == jnp.where(w == 0, prior, seg_last)
        g = gloc[w] + jnp.where(kept, gacc[w], 0.0)
        gsc[w, 0], gsc[w, 1] = g[:, :half], g[:, half:]
        c_copy(w).start()

    def reduce_rows(w):
        c_copy(w).wait_recv()
        v = gsc[w, core] + grc[w]
        top = jnp.max(jnp.abs(v), axis=0, keepdims=True)
        power = jnp.ceil(jnp.log2(jnp.maximum(top, 1e-30)))
        code = jnp.round(v * (jnp.exp2(-power) * 32000.0))
        hx[w, yy, :state] = code.astype(jnp.int32).astype(jnp.int16)
        hx[w, yy, state:] = (
            jnp.broadcast_to(power, (16, half)).astype(jnp.int32).astype(jnp.int16)
        )
        for d in range(1, ny):
            y_copy(w, d, yy).start()

    def reduce_end(w):
        for d in range(1, ny):
            y_copy(w, d, lax.rem(yy + ny - d, ny)).wait_recv()
        total = jnp.zeros((state, half), F32)
        for j in range(ny):
            power = hx[w, j, state:].astype(jnp.int32).astype(F32)[0:1]
            code = hx[w, j, :state].astype(jnp.int32).astype(F32)
            total = total + code * (jnp.exp2(power) * (1.0 / 32000.0))
        gfin[w, core] = total.T.astype(BF16)
        f_copy(w, core).start()

    @pl.loop(0, GROUP)
    def _(k):
        @pl.when(k == 0)
        def _():
            p_copy().wait_recv()

        @pl.when(jnp.logical_not(can_take(early)))
        def _():
            handle(early, k)

        p2(k)

    @pl.loop(0, GROUP)
    def _(k):
        @pl.when(can_take(early))
        def _():
            handle(early, k)

        p2(GROUP + k)

    @pl.loop(0, GROUP)
    def _(k):
        @pl.when(can_send(late))
        def _():
            handle(late, k)

        p3(early, x * GROUP + k)

    mixed = split(jnp.where(same & (r_id >= c_id), macc[...], 0.0))
    gloc[0] = (mm(mixed[0], keys) + mm(mixed[1], keys)).T
    gloc[1] = (mm(mixed[0], queries, 0, 0) + mm(mixed[1], queries, 0, 0)).T

    @pl.loop(0, GROUP)
    def _(k):
        p3_taken(early, k)

        @pl.when(jnp.logical_not(can_send(late)))
        def _():
            handle(late, k)

    reduce_core(early)

    @pl.loop(0, GROUP)
    def _(k):
        p3(late, x * GROUP + k)

    reduce_rows(early)

    @pl.loop(0, GROUP)
    def _(k):
        p3_taken(late, k)

    reduce_core(late)
    reduce_end(early)
    reduce_rows(late)
    reduce_end(late)
    for w in range(2):
        f_copy(w, 1 - core).wait_recv()
    for j in range(2):
        gq_ref[j * half : (j + 1) * half] = gfin[0, j]
        gk_ref[j * half : (j + 1) * half] = gfin[1, j]

    p_copy().wait_send()
    for w in range(2):
        c_copy(w).wait_send()
        f_copy(w, core).wait_send()
        for d in range(1, ny):
            y_copy(w, d, yy).wait_send()

        @pl.loop(0, GROUP)
        def _(k):
            x_copy(w, k).wait_send()
            t_copy(w, k).wait_send()

            @pl.when(can_send(w))
            def _():
                z_copy(w, k).wait_send()


def solution(mesh):
    nseq, nhead = mesh.shape["seq"], mesh.shape["head"]

    def on_device(signal, step_raw, key_proj, query_proj, decay_log, skip_gain, lengths, cotangent):
        tok, heads, width = signal.shape
        state = key_proj.shape[1]
        blocks = 2 * GROUP
        hb = heads // blocks
        rows = hb * width
        half = tok // 2
        ny = nhead // 2
        dma = pltpu.SemaphoreType.DMA
        vmem = pltpu.VMEM
        st = (hb, width, state)
        scratch = (
            [vmem((2, heads, width, tok), BF16)]
            + [vmem((2, blocks, rows, tok), BF16)] * 2
            + [vmem((2, blocks, rows, tok), F32)]
            + [vmem((tok, tok), F32)]
            + [vmem((tok, tok), BF16)] * 4
            + [vmem((2, tok, 2 * state), BF16)]
            + [vmem((2, blocks, hb, tok), F32)]
            + [vmem((blocks, hb, state), F32)] * 2
            + [vmem((2, blocks, hb, state), F32)]
            + [vmem((blocks, hb, state), F32)]
            + [vmem((2, blocks) + st, F32)] * 2
            + [vmem((2, GROUP, rows + 16, state), jnp.int16)] * 6
            + [vmem((2, state, tok), F32)] * 2
            + [vmem((2, 2, state, half), F32)]
            + [vmem((2, state, half), F32)]
            + [vmem((2, ny, state + 16, half), jnp.int16)]
            + [vmem((2, 2, half, state), BF16)]
            + [dma((2, 2)), dma((2,))]
            + [dma((2, 2, GROUP))] * 3
            + [dma((2, 2)), dma((2, 2, ny)), dma((2, 2))]
        )
        turned = jax.ShapeDtypeStruct((2, heads, width, tok), BF16)
        grads = jax.ShapeDtypeStruct((tok, state), BF16)
        whole = pl.BlockSpec(memory_space=pltpu.VMEM)
        anywhere = pl.BlockSpec(memory_space=pl.ANY)
        res, gk, gq = pl.pallas_call(
            functools.partial(kernel, nseq, nhead),
            out_shape=(turned, grads, grads),
            in_specs=[pl.BlockSpec(memory_space=pltpu.SMEM)] + [anywhere] * 2 + [whole] * 5,
            out_specs=(whole,) * 3,
            scratch_shapes=scratch,
            compiler_params=pltpu.CompilerParams(
                collective_id=0, has_side_effects=True, vmem_limit_bytes=60 << 20
            ),
        )(
            lengths,
            jnp.transpose(signal, (1, 2, 0)),
            jnp.transpose(cotangent, (1, 2, 0)),
            step_raw.T,
            key_proj,
            query_proj,
            decay_log[None, :],
            skip_gain[None, :],
        )
        return jnp.transpose(res[0], (2, 0, 1)), jnp.transpose(res[1], (2, 0, 1)), gk, gq

    in_specs = (
        P("seq", "head", None),
        P("seq", "head"),
        P("seq", None),
        P("seq", None),
        P("head"),
        P("head"),
        P(),
        P("seq", "head", None),
    )
    out_specs = (P("seq", "head", None), P("seq", "head", None), P("seq", None), P("seq", None))
    return jax.shard_map(
        on_device, mesh=mesh, in_specs=in_specs, out_specs=out_specs, check_vma=False
    )
```

```python
import functools

import jax
import jax.numpy as jnp
from jax import lax
from jax.experimental import pallas as pl
from jax.experimental.pallas import tpu as pltpu
from jax.sharding import PartitionSpec as P

MESH = pl.DeviceIdType.MESH
F32 = jnp.float32
BF16 = jnp.bfloat16
GROUP = 4


def mm(a, b, ca=1, cb=0):
    return lax.dot_general(a, b, (((ca,), (cb,)), ((), ())), preferred_element_type=F32)


def split(a):
    hi = a.astype(BF16)
    return hi, (a - hi.astype(F32)).astype(BF16)


def mm3(a, b, ca=1, cb=0):
    return mm(a[0], b[0], ca, cb) + mm(a[0], b[1], ca, cb) + mm(a[1], b[0], ca, cb)


def put(ref, w, k, v):
    hb, width, state = v.shape
    top = jnp.max(jnp.abs(v), axis=1)
    power = jnp.ceil(jnp.log2(jnp.maximum(top, 1e-30)))
    code = jnp.round(v * (jnp.exp2(-power) * 32000.0)[:, None, :])
    ref[w, k, : hb * width] = code.reshape(hb * width, state).astype(jnp.int32).astype(jnp.int16)
    pad = jnp.concatenate([power, jnp.zeros((16 - hb, state), F32)], axis=0)
    ref[w, k, hb * width :] = pad.astype(jnp.int32).astype(jnp.int16)


def get(ref, w, k, hb, width, state):
    power = ref[w, k, hb * width :].astype(jnp.int32).astype(F32)[:hb]
    code = ref[w, k, : hb * width].astype(jnp.int32).astype(F32).reshape(hb, width, state)
    return code * (jnp.exp2(power) * (1.0 / 32000.0))[:, None, :]


def kernel(
    nseq, nhead, len_ref, sig, cot, step_ref, key_ref, query_ref, dl_ref, sk_ref,
    res_ref, gk_ref, gq_ref,
    inp, hi, lo, ys, macc, gh, gl, gth, gtl, proj, fac, pas, pasr, scl, skp, loc, ins,
    xq, xr, zq, zr, tq, tr, gacc, gloc, gsc, grc, hx, gfin,
    isem, psem, xsem, zsem, tsem, csem, ysem, fsem,
):
    _, heads, width, tok = inp.shape
    state = key_ref.shape[1]
    blocks = 2 * GROUP
    hb = heads // blocks
    rows = hb * width
    half = tok // 2
    ny = nhead // 2
    me, hd = lax.axis_index("seq"), lax.axis_index("head")
    x, z = lax.rem(me, 2), me // 2
    yy, core = hd // 2, lax.rem(hd, 2)
    nz = nseq // 2
    partner = me + 1 - 2 * x
    mate = hd + 1 - 2 * core
    early = jnp.where(z < nz // 2, 0, 1)
    late = 1 - early

    def can_take(w):
        return jnp.where(w == 0, z, nz - 1 - z) > 0

    def can_send(w):
        return jnp.where(w == 0, nz - 1 - z, z) > 0

    sides = (1 - x, x)

    def in_copy(src, w, j):
        part = pl.ds(sides[j] * (heads // 2), heads // 2)
        return pltpu.make_async_copy(src.at[part], inp.at[w, part], isem.at[w, j])

    for j in range(2):
        in_copy(sig, 0, j).start()
        in_copy(cot, 1, j).start()

    barrier = pltpu.get_barrier_semaphore()

    def greet(seq, head):
        pl.semaphore_signal(barrier, inc=1, device_id=(seq, head), device_id_type=MESH)

    greet(partner, hd)

    @pl.when(z > 0)
    def _():
        greet(me - 2, hd)

    @pl.when(z < nz - 1)
    def _():
        greet(me + 2, hd)

    greet(me, mate)
    for d in range(1, ny):
        greet(me, lax.rem(hd + 2 * d, nhead))

    def hblock(b):
        return pl.ds(b * hb, hb)

    def rcopy(src, dst, sems, index, seq, head=None):
        return pltpu.make_async_remote_copy(
            src_ref=src, dst_ref=dst, send_sem=sems.at[(0,) + index], recv_sem=sems.at[(1,) + index],
            device_id=(seq, hd if head is None else head), device_id_type=MESH,
        )

    def p_copy():
        return rcopy(pas, pasr, psem, (), partner)

    def x_copy(w, k):
        return rcopy(xq.at[w, k], xr.at[w, k], xsem, (w, k), partner)

    def z_copy(w, k):
        return rcopy(zq.at[w, k], zr.at[w, k], zsem, (w, k), me + 2 - 4 * w)

    def t_copy(w, k):
        return rcopy(tq.at[w, k], tr.at[w, k], tsem, (w, k), partner)

    start = me * tok
    end, ends = jnp.int32(0), []
    for k in range(len_ref.shape[0]):
        end = end + len_ref[k]
        ends.append(end)

    def segment(places):
        total = jnp.zeros_like(places)
        for value in ends:
            total = total + jnp.where(places >= value, 1, 0)
        return total

    seg_last = segment(start + tok - 1)
    prior = jnp.where(start > 0, segment(start - 1), -1)
    seg_col = segment(start + lax.broadcasted_iota(jnp.int32, (tok, 1), 0))
    seg_row = segment(start + lax.broadcasted_iota(jnp.int32, (1, tok), 1))
    r_id = lax.broadcasted_iota(jnp.int32, (tok, tok), 0)
    c_id = lax.broadcasted_iota(jnp.int32, (tok, tok), 1)
    upper = jnp.where(r_id <= c_id, 1.0, 0.0).astype(BF16)

    raw = step_ref[...].astype(F32)
    size = jnp.maximum(raw, 0.0) + jnp.log1p(jnp.exp(-jnp.abs(raw)))
    eye = lax.broadcasted_iota(jnp.int32, (heads, heads), 0) == lax.broadcasted_iota(
        jnp.int32, (heads, heads), 1
    )
    column = lambda ref: jnp.sum(jnp.where(eye, ref[...], 0.0), axis=1, keepdims=True)
    logdec = size * (-jnp.exp(column(dl_ref)))
    one = logdec.astype(BF16)
    rest = logdec - one.astype(F32)
    two, three = split(rest)
    cum = mm(three, upper) + mm(two, upper) + mm(one, upper)
    mid, final = cum[:, half - 1 : half], cum[:, tok - 1 : tok]
    e = jnp.exp(cum - mid)
    f = size * jnp.exp(mid - cum)
    lanes = (heads, state)
    passing = jnp.broadcast_to(jnp.where(seg_last == prior, jnp.exp(final), 0.0), lanes)
    to_last = jnp.broadcast_to(jnp.exp(final - mid), lanes)
    to_mid = jnp.broadcast_to(jnp.exp(mid), lanes)
    skips = jnp.broadcast_to(column(sk_ref), lanes)
    for b in range(blocks):
        part = slice(b * hb, (b + 1) * hb)
        fac[0, b], fac[1, b] = f[part], e[part]
        scl[0, b], scl[1, b] = to_last[part], to_mid[part]
        pas[b], skp[b] = passing[part], skips[part]

    keys, queries = key_ref[...], query_ref[...]
    km = jnp.where(seg_col == seg_last, keys.astype(F32), 0.0).astype(BF16)
    qm = jnp.where(seg_col == prior, queries.astype(F32), 0.0).astype(BF16)
    for j in range(2):
        proj[0, :, j * state : (j + 1) * state] = km
        proj[1, :, j * state : (j + 1) * state] = qm

    for w in range(2):
        @pl.when(jnp.logical_not(can_take(w)))
        def _():
            zr[w] = jnp.zeros_like(zr[w])

    pl.semaphore_wait(
        barrier, 1 + ny + jnp.where(z > 0, 1, 0) + jnp.where(z < nz - 1, 1, 0)
    )
    p_copy().start()

    def p1(w, b):
        t = inp[w, hblock(b)].astype(F32) * fac[w, b][:, None, :]
        top, low = split(t.reshape(rows, tok))
        hi[w, b], lo[w, b] = top, low
        pr = proj[w, :, :state]
        return (mm(top, pr) + mm(low, pr)).reshape(hb, width, state) * scl[w, b][:, None, :]

    for w in (early, late):
        in_copy(sig, w, 0).wait()

        @pl.loop(0, GROUP)
        def _(k):
            put(xq, w, k, p1(w, (1 - x) * GROUP + k))
            x_copy(w, k).start()

    for w in (early, late):
        in_copy(sig, w, 1).wait()

        @pl.loop(0, GROUP)
        def _(k):
            b = x * GROUP + k
            loc[w, b] = p1(w, b)

    same = seg_col == seg_row
    gram = jnp.where(same & (r_id >= c_id), mm(queries, keys, 1, 1), 0.0)
    gh[...], gl[...] = split(gram)
    gram_t = jnp.where(same & (r_id <= c_id), mm(keys, queries, 1, 1), 0.0)
    gth[...], gtl[...] = split(gram_t)
    macc[...] = jnp.zeros_like(macc)
    gacc[...] = jnp.zeros_like(gacc)

    def p2(b):
        bb = (hi[0, b], lo[0, b])
        aa = (hi[1, b], lo[1, b])
        b0 = (bb[0][:, :half], bb[1][:, :half])
        a0 = (aa[0][:, :half], aa[1][:, :half])
        a1 = (aa[0][:, half:], aa[1][:, half:])
        ys[0, b, :, :half] = mm3(b0, (gth[:half, :half], gtl[:half, :half]))
        ys[0, b, :, half:] = mm3(bb, (gth[:, half:], gtl[:, half:]))
        ys[1, b, :, half:] = mm3(a1, (gh[half:, half:], gl[half:, half:]))
        ys[1, b, :, :half] = mm3(aa, (gh[:, :half], gl[:, :half]))
        macc[:half, :half] += mm3(a0, b0, 0, 0)
        macc[half:, :] += mm3(a1, bb, 0, 0)

    def handle(w, k):
        b = x * GROUP + k
        first = x == w
        x_copy(w, k).wait_recv()

        @pl.when(can_take(w))
        def _():
            z_copy(w, k).wait_recv()

        own, other = pas[b][:, None, :], pasr[b][:, None, :]
        mine, theirs = loc[w, b], get(xr, w, k, hb, width, state)
        pass0, pass1 = jnp.where(first, own, other), jnp.where(first, other, own)
        loc0, loc1 = jnp.where(first, mine, theirs), jnp.where(first, theirs, mine)
        in0 = get(zr, w, k, hb, width, state)
        in1 = pass0 * in0 + loc0

        @pl.when(can_send(w))
        def _():
            put(zq, w, k, pass1 * in1 + loc1)
            z_copy(w, k).start()

        put(tq, w, k, jnp.where(first, in1, in0))
        t_copy(w, k).start()
        ins[w, b] = jnp.where(first, in0, in1)

    def p3(w, b):
        st = split((ins[w, b] * scl[1 - w, b][:, None, :]).reshape(rows, state))
        both = jnp.concatenate(st, axis=1)
        m = mm(both, hi[1 - w, b], 0, 0)
        gacc[w] += m[:state] + m[state:] + mm(st[0], lo[1 - w, b], 0, 0)
        y = ys[w, b] + mm(both, proj[1 - w], 1, 1)
        skip = skp[b][:, 0:1][:, :, None]
        res_ref[w, hblock(b)] = (
            y.reshape(hb, width, tok) * fac[1 - w, b][:, None, :]
            + skip * inp[w, hblock(b)].astype(F32)
        ).astype(BF16)

    def p3_taken(w, k):
        t_copy(w, k).wait_recv()
        b = (1 - x) * GROUP + k
        ins[w, b] = get(tr, w, k, hb, width, state)
        p3(w, b)

    def c_copy(w):
        return rcopy(gsc.at[w, 1 - core], grc.at[w], csem, (w,), me, mate)

    def y_copy(w, d, slot):
        return rcopy(hx.at[w, slot], hx.at[w, slot], ysem, (w, d), me, lax.rem(hd + 2 * d, nhead))

    def f_copy(w, slot):
        return rcopy(gfin.at[w, slot], gfin.at[w, slot], fsem, (w,), me, mate)

    def reduce_core(w):
        kept = seg_row == jnp.where(w == 0, prior, seg_last)
        g = gloc[w] + jnp.where(kept, gacc[w], 0.0)
        gsc[w, 0], gsc[w, 1] = g[:, :half], g[:, half:]
        c_copy(w).start()

    def reduce_rows(w):
        c_copy(w).wait_recv()
        v = gsc[w, core] + grc[w]
        top = jnp.max(jnp.abs(v), axis=0, keepdims=True)
        power = jnp.ceil(jnp.log2(jnp.maximum(top, 1e-30)))
        code = jnp.round(v * (jnp.exp2(-power) * 32000.0))
        hx[w, yy, :state] = code.astype(jnp.int32).astype(jnp.int16)
        hx[w, yy, state:] = (
            jnp.broadcast_to(power, (16, half)).astype(jnp.int32).astype(jnp.int16)
        )
        for d in range(1, ny):
            y_copy(w, d, yy).start()

    def reduce_end(w):
        for d in range(1, ny):
            y_copy(w, d, lax.rem(yy + ny - d, ny)).wait_recv()
        total = jnp.zeros((state, half), F32)
        for j in range(ny):
            power = hx[w, j, state:].astype(jnp.int32).astype(F32)[0:1]
            code = hx[w, j, :state].astype(jnp.int32).astype(F32)
            total = total + code * (jnp.exp2(power) * (1.0 / 32000.0))
        gfin[w, core] = total.T.astype(BF16)
        f_copy(w, core).start()

    @pl.loop(0, GROUP)
    def _(k):
        @pl.when(k == 0)
        def _():
            p_copy().wait_recv()

        @pl.when(jnp.logical_not(can_take(early)))
        def _():
            handle(early, k)

        p2(k)

    @pl.loop(0, GROUP)
    def _(k):
        @pl.when(can_take(early))
        def _():
            handle(early, k)

        p2(GROUP + k)

    @pl.loop(0, GROUP)
    def _(k):
        @pl.when(can_send(late))
        def _():
            handle(late, k)

        p3(early, x * GROUP + k)

    mixed = split(jnp.where(same & (r_id >= c_id), macc[...], 0.0))
    gloc[0] = (mm(mixed[0], keys) + mm(mixed[1], keys)).T
    gloc[1] = (mm(mixed[0], queries, 0, 0) + mm(mixed[1], queries, 0, 0)).T

    @pl.loop(0, GROUP)
    def _(k):
        p3_taken(early, k)

        @pl.when(jnp.logical_not(can_send(late)))
        def _():
            handle(late, k)

    reduce_core(early)

    @pl.loop(0, GROUP)
    def _(k):
        p3(late, x * GROUP + k)

    reduce_rows(early)

    @pl.loop(0, GROUP)
    def _(k):
        p3_taken(late, k)

    reduce_core(late)
    reduce_end(early)
    reduce_rows(late)
    reduce_end(late)
    for w in range(2):
        f_copy(w, 1 - core).wait_recv()
    for j in range(2):
        gq_ref[j * half : (j + 1) * half] = gfin[0, j]
        gk_ref[j * half : (j + 1) * half] = gfin[1, j]

    p_copy().wait_send()
    for w in range(2):
        c_copy(w).wait_send()
        f_copy(w, core).wait_send()
        for d in range(1, ny):
            y_copy(w, d, yy).wait_send()

        @pl.loop(0, GROUP)
        def _(k):
            x_copy(w, k).wait_send()
            t_copy(w, k).wait_send()

            @pl.when(can_send(w))
            def _():
                z_copy(w, k).wait_send()


def store(res, gk, gq, out_ref, gs_ref, gk_ref, gq_ref, sems):
    pairs = ((res.at[0], out_ref), (res.at[1], gs_ref), (gk, gk_ref), (gq, gq_ref))
    copies = [pltpu.make_async_copy(a, b, sems.at[i]) for i, (a, b) in enumerate(pairs)]
    for copy in copies:
        copy.start()
    for copy in copies:
        copy.wait()


def solution(mesh):
    nseq, nhead = mesh.shape["seq"], mesh.shape["head"]

    def on_device(signal, step_raw, key_proj, query_proj, decay_log, skip_gain, lengths, cotangent):
        tok, heads, width = signal.shape
        state = key_proj.shape[1]
        blocks = 2 * GROUP
        hb = heads // blocks
        rows = hb * width
        half = tok // 2
        ny = nhead // 2
        dma = pltpu.SemaphoreType.DMA
        vmem = pltpu.VMEM
        st = (hb, width, state)
        scratch = (
            [vmem((2, heads, width, tok), BF16)]
            + [vmem((2, blocks, rows, tok), BF16)] * 2
            + [vmem((2, blocks, rows, tok), F32)]
            + [vmem((tok, tok), F32)]
            + [vmem((tok, tok), BF16)] * 4
            + [vmem((2, tok, 2 * state), BF16)]
            + [vmem((2, blocks, hb, tok), F32)]
            + [vmem((blocks, hb, state), F32)] * 2
            + [vmem((2, blocks, hb, state), F32)]
            + [vmem((blocks, hb, state), F32)]
            + [vmem((2, blocks) + st, F32)] * 2
            + [vmem((2, GROUP, rows + 16, state), jnp.int16)] * 6
            + [vmem((2, state, tok), F32)] * 2
            + [vmem((2, 2, state, half), F32)]
            + [vmem((2, state, half), F32)]
            + [vmem((2, ny, state + 16, half), jnp.int16)]
            + [vmem((2, 2, half, state), BF16)]
            + [dma((2, 2)), dma((2,))]
            + [dma((2, 2, GROUP))] * 3
            + [dma((2, 2)), dma((2, 2, ny)), dma((2, 2))]
        )
        turned = jax.ShapeDtypeStruct((heads, width, tok), BF16)
        grads = jax.ShapeDtypeStruct((tok, state), BF16)
        whole = pl.BlockSpec(memory_space=pltpu.VMEM)
        anywhere = pl.BlockSpec(memory_space=pl.ANY)
        res, gk, gq = pl.pallas_call(
            functools.partial(kernel, nseq, nhead),
            out_shape=(
                vmem((2, heads, width, tok), BF16), vmem((tok, state), BF16), vmem((tok, state), BF16)
            ),
            in_specs=[pl.BlockSpec(memory_space=pltpu.SMEM)] + [anywhere] * 2 + [whole] * 5,
            out_specs=(whole,) * 3,
            scratch_shapes=scratch,
            compiler_params=pltpu.CompilerParams(
                collective_id=0, has_side_effects=True, vmem_limit_bytes=58 << 20
            ),
        )(
            lengths,
            jnp.transpose(signal, (1, 2, 0)),
            jnp.transpose(cotangent, (1, 2, 0)),
            step_raw.T,
            key_proj,
            query_proj,
            decay_log[None, :],
            skip_gain[None, :],
        )
        out, gs, gk, gq = pl.pallas_call(
            store,
            out_shape=(turned, turned, grads, grads),
            in_specs=[whole] * 3,
            out_specs=(anywhere,) * 4,
            scratch_shapes=[dma((4,))],
            compiler_params=pltpu.CompilerParams(vmem_limit_bytes=2 << 20),
        )(*(pltpu.with_memory_space_constraint(v, pltpu.VMEM) for v in (res, gk, gq)))
        return jnp.transpose(out, (2, 0, 1)), jnp.transpose(gs, (2, 0, 1)), gk, gq

    in_specs = (
        P("seq", "head", None),
        P("seq", "head"),
        P("seq", None),
        P("seq", None),
        P("head"),
        P("head"),
        P(),
        P("seq", "head", None),
    )
    out_specs = (P("seq", "head", None), P("seq", "head", None), P("seq", None), P("seq", None))
    return jax.shard_map(
        on_device, mesh=mesh, in_specs=in_specs, out_specs=out_specs, check_vma=False
    )
```

```python
import functools

import jax
import jax.numpy as jnp
from jax import lax
from jax.experimental import pallas as pl
from jax.experimental.pallas import tpu as pltpu
from jax.sharding import PartitionSpec as P

MESH = pl.DeviceIdType.MESH
F32 = jnp.float32
BF16 = jnp.bfloat16
GROUP = 4


def mm(a, b, ca=1, cb=0):
    return lax.dot_general(a, b, (((ca,), (cb,)), ((), ())), preferred_element_type=F32)


def split(a):
    hi = a.astype(BF16)
    return hi, (a - hi.astype(F32)).astype(BF16)


def mm3(a, b, ca=1, cb=0):
    return mm(a[0], b[0], ca, cb) + mm(a[0], b[1], ca, cb) + mm(a[1], b[0], ca, cb)


def put(ref, w, c, v):
    heads, width, state = v.shape
    top = jnp.max(jnp.abs(v), axis=1)
    power = jnp.ceil(jnp.log2(jnp.maximum(top, 1e-30)))
    code = jnp.round(v * (jnp.exp2(-power) * 32000.0)[:, None, :])
    ref[w, c, : heads * width] = code.reshape(heads * width, state).astype(jnp.int32).astype(jnp.int16)
    pad = jnp.concatenate([power, jnp.zeros((16 - heads, state), F32)], axis=0)
    ref[w, c, heads * width :] = pad.astype(jnp.int32).astype(jnp.int16)


def get(ref, w, c, shape):
    heads, width, state = shape
    power = ref[w, c, heads * width :].astype(jnp.int32).astype(F32)[:heads]
    code = ref[w, c, : heads * width].astype(jnp.int32).astype(F32).reshape(shape)
    return code * (jnp.exp2(power) * (1.0 / 32000.0))[:, None, :]


def kernel(
    nseq, nhead, len_in, sig, cot, step_in, key_in, query_in, dl_in, sk_in,
    res_ref, gk_ref, gq_ref,
    len_ref, step_ref, key_ref, query_ref, dl_ref, sk_ref, inp, hi, lo, ys, macc, gh, gl, gth, gtl, proj, tall, fac, pas, pasr, scl, skp, loc, ins,
    xq, xr, zq, zr, tq, tr, gacc, gloc, gsc, grc, hx, gfin,
    ssem, isem, psem, xsem, zsem, tsem, csem, ysem, fsem,
):
    _, heads, width, tok = inp.shape
    state = key_ref.shape[1]
    blocks = 2 * GROUP
    hb = heads // blocks
    rows = hb * width
    cuts = 1
    hc = hb // cuts
    piece = (hc, width, state)
    half = tok // 2
    ny = nhead // 2
    me, hd = lax.axis_index("seq"), lax.axis_index("head")
    x, z = lax.rem(me, 2), me // 2
    yy, core = hd // 2, lax.rem(hd, 2)
    nz = nseq // 2
    partner = me + 1 - 2 * x
    mate = hd + 1 - 2 * core
    early = jnp.where(z < nz // 2, 0, 1)
    late = 1 - early

    barrier = pltpu.get_barrier_semaphore()

    def greet(seq, head):
        pl.semaphore_signal(barrier, inc=1, device_id=(seq, head), device_id_type=MESH)

    greet(partner, hd)

    @pl.when(z > 0)
    def _():
        greet(me - 2, hd)

    @pl.when(z < nz - 1)
    def _():
        greet(me + 2, hd)

    greet(me, mate)
    for d in range(1, ny):
        greet(me, lax.rem(hd + 2 * d, nhead))

    small = [
        pltpu.make_async_copy(a, b, ssem.at[n])
        for n, (a, b) in enumerate(
            (
                (step_in, step_ref), (dl_in, dl_ref), (len_in, len_ref), (key_in, key_ref),
                (query_in, query_ref), (sk_in, sk_ref),
            )
        )
    ]
    for copy in small:
        copy.start()

    sides = (1 - x, x)

    def hblock(b):
        return pl.ds(b * hb, hb)

    def in_copy(src, w, j, k, size):
        part = pl.ds((sides[j] * GROUP + k) * hb, size * hb)
        return pltpu.make_async_copy(src.at[part], inp.at[w, part], isem.at[w, j, 1 if k else 0])

    def fetch(w, j, k, size):
        @pl.when(w == 0)
        def _():
            in_copy(sig, 0, j, k, size).start()

        @pl.when(w == 1)
        def _():
            in_copy(cot, 1, j, k, size).start()

    fetch(early, 0, 0, 1)

    def rcopy(src, dst, sems, index, seq, head=None):
        return pltpu.make_async_remote_copy(
            src_ref=src, dst_ref=dst, send_sem=sems.at[(0,) + index], recv_sem=sems.at[(1,) + index],
            device_id=(seq, hd if head is None else head), device_id_type=MESH,
        )

    def p_copy():
        return rcopy(pas, pasr, psem, (), partner)

    def x_copy(w, c):
        return rcopy(xq.at[w, c], xr.at[w, c], xsem, (w, c), partner)

    def z_copy(w, c):
        return rcopy(zq.at[w, c], zr.at[w, c], zsem, (w, c), me + 2 - 4 * w)

    def t_copy(w, c):
        return rcopy(tq.at[w, c], tr.at[w, c], tsem, (w, c), partner)

    def cut(i):
        return slice(i * hc, (i + 1) * hc)

    rank = jnp.where(early == 0, z, nz - 1 - z)
    edge = rank == 0
    leads_early, leads_late = x == early, x == late

    for copy in small:
        copy.wait()

    start = me * tok
    end, ends = jnp.int32(0), []
    for k in range(len_ref.shape[0]):
        end = end + len_ref[k]
        ends.append(end)

    def segment(places):
        total = jnp.zeros_like(places)
        for value in ends:
            total = total + jnp.where(places >= value, 1, 0)
        return total

    seg_last = segment(start + tok - 1)
    prior = jnp.where(start > 0, segment(start - 1), -1)
    seg_col = segment(start + lax.broadcasted_iota(jnp.int32, (tok, 1), 0))
    seg_row = segment(start + lax.broadcasted_iota(jnp.int32, (1, tok), 1))
    upper = jnp.where(
        lax.broadcasted_iota(jnp.int32, (half, half), 0)
        <= lax.broadcasted_iota(jnp.int32, (half, half), 1),
        1.0,
        0.0,
    ).astype(BF16)

    raw = step_ref[...].astype(F32)
    size = jnp.maximum(raw, 0.0) + jnp.log1p(jnp.exp(-jnp.abs(raw)))
    eye = lax.broadcasted_iota(jnp.int32, (heads, heads), 0) == lax.broadcasted_iota(
        jnp.int32, (heads, heads), 1
    )
    column = lambda ref: jnp.sum(jnp.where(eye, ref[...], 0.0), axis=1, keepdims=True)
    logdec = size * (-jnp.exp(column(dl_ref)))
    one = logdec.astype(BF16)
    rest = logdec - one.astype(F32)
    two, three = split(rest)
    parts = [p[:, j * half : (j + 1) * half] for j in range(2) for p in (one, two, three)]
    sums = mm(jnp.concatenate(parts, axis=0), upper)
    sums = [sums[i * heads : (i + 1) * heads] for i in range(6)]
    cum0 = sums[2] + sums[1] + sums[0]
    mid = cum0[:, half - 1 : half]
    cum = jnp.concatenate([cum0, sums[5] + sums[4] + sums[3] + mid], axis=1)
    final = cum[:, tok - 1 : tok]
    e = jnp.exp(cum - mid)
    f = size * jnp.exp(mid - cum)
    lanes = (heads, state)
    passing = jnp.broadcast_to(jnp.where(seg_last == prior, jnp.exp(final), 0.0), lanes)
    to_last = jnp.broadcast_to(jnp.exp(final - mid), lanes)
    to_mid = jnp.broadcast_to(jnp.exp(mid), lanes)
    skips = jnp.broadcast_to(column(sk_ref), lanes)
    for b in range(blocks):
        part = slice(b * hb, (b + 1) * hb)
        fac[0, b], fac[1, b] = f[part], e[part]
        scl[0, b], scl[1, b] = to_last[part], to_mid[part]
        pas[b], skp[b] = passing[part], skips[part]

    keys, queries = key_ref[...], query_ref[...]
    km = jnp.where(seg_col == seg_last, keys.astype(F32), 0.0).astype(BF16)
    qm = jnp.where(seg_col == prior, queries.astype(F32), 0.0).astype(BF16)
    for j in range(2):
        proj[0, :, j * state : (j + 1) * state] = km
        proj[1, :, j * state : (j + 1) * state] = qm
        tall[0, j * tok : (j + 1) * tok] = km
        tall[1, j * tok : (j + 1) * tok] = qm

    fetch(early, 0, 1, GROUP - 1)
    fetch(late, 0, 0, GROUP)
    fetch(early, 1, 0, GROUP)
    fetch(late, 1, 0, GROUP)

    pl.semaphore_wait(
        barrier, 1 + ny + jnp.where(z > 0, 1, 0) + jnp.where(z < nz - 1, 1, 0)
    )
    p_copy().start()

    def p1(w, b):
        t = inp[w, hblock(b)].astype(F32) * fac[w, b][:, None, :]
        top, low = split(t.reshape(rows, tok))
        hi[w, b], lo[w, b] = top, low
        both = jnp.concatenate([top, low], axis=1)
        return mm(both, tall[w]).reshape(hb, width, state) * scl[w, b][:, None, :]

    in_copy(sig, early, 0, 0, 1).wait()
    for w in (early, late):
        if w is late:
            in_copy(sig, late, 0, 0, GROUP).wait()

        @pl.loop(0, GROUP)
        def _(k):
            if w is early:
                @pl.when(k == 1)
                def _():
                    in_copy(sig, early, 0, 1, GROUP - 1).wait()

            value = p1(w, (1 - x) * GROUP + k)
            for i in range(cuts):
                c = k * cuts + i
                put(xq, w, c, value[cut(i)])
                if w is early:
                    x_copy(w, c).start()
                else:
                    @pl.when(jnp.logical_not(edge) | leads_late)
                    def _():
                        x_copy(w, c).start()

    for w in (early, late):
        in_copy(sig, w, 1, 0, GROUP).wait()

        @pl.loop(0, GROUP)
        def _(k):
            b = x * GROUP + k
            loc[w, b] = p1(w, b)

    r_id = lax.broadcasted_iota(jnp.int32, (tok, tok), 0)
    c_id = lax.broadcasted_iota(jnp.int32, (tok, tok), 1)
    same = seg_col == seg_row
    gram = jnp.where(same & (r_id >= c_id), mm(queries, keys, 1, 1), 0.0)
    gh[...], gl[...] = split(gram)
    gram_t = jnp.where(same & (r_id <= c_id), mm(keys, queries, 1, 1), 0.0)
    gth[...], gtl[...] = split(gram_t)
    macc[...] = jnp.zeros_like(macc)
    gacc[...] = jnp.zeros_like(gacc)

    def pair(ref, w, k):
        return ref[w, pl.ds(2 * k, 2)].reshape(2 * rows, tok)

    def p2_out(k):
        bb = (pair(hi, 0, k), pair(lo, 0, k))
        b0 = (bb[0][:, :half], bb[1][:, :half])
        left = mm3(b0, (gth[:half, :half], gtl[:half, :half]))
        ys[0, pl.ds(2 * k, 2), :, :half] = left.reshape(2, rows, half)
        right = mm3(bb, (gth[:, half:], gtl[:, half:]))
        ys[0, pl.ds(2 * k, 2), :, half:] = right.reshape(2, rows, half)

    def p2_grad(k):
        aa = (pair(hi, 1, k), pair(lo, 1, k))
        a1 = (aa[0][:, half:], aa[1][:, half:])
        right = mm3(a1, (gh[half:, half:], gl[half:, half:]))
        ys[1, pl.ds(2 * k, 2), :, half:] = right.reshape(2, rows, half)
        left = mm3(aa, (gh[:, :half], gl[:, :half]))
        ys[1, pl.ds(2 * k, 2), :, :half] = left.reshape(2, rows, half)

    def p2_mix(b):
        bb = (hi[0, b], lo[0, b])
        aa = (hi[1, b], lo[1, b])
        b0 = (bb[0][:, :half], bb[1][:, :half])
        a0 = (aa[0][:, :half], aa[1][:, :half])
        a1 = (aa[0][:, half:], aa[1][:, half:])
        macc[:half, :half] += mm3(a0, b0, 0, 0)
        macc[half:, :] += mm3(a1, bb, 0, 0)

    def handle(w, k, i, sends, takes):
        b, c, part = x * GROUP + k, k * cuts + i, cut(i)
        first = x == w
        if sends:
            x_copy(w, c).wait_recv()
        else:
            @pl.when(jnp.logical_not(first))
            def _():
                x_copy(w, c).wait_recv()

        if takes:
            z_copy(w, c).wait_recv()

        own, other = pas[b, part][:, None, :], pasr[b, part][:, None, :]
        mine, theirs = loc[w, b, part], get(xr, w, c, piece)
        pass0, pass1 = jnp.where(first, own, other), jnp.where(first, other, own)
        loc0, loc1 = jnp.where(first, mine, theirs), jnp.where(first, theirs, mine)
        in0 = get(zr, w, c, piece) if takes else jnp.zeros_like(mine)
        in1 = pass0 * in0 + loc0
        if sends:
            put(zq, w, c, pass1 * in1 + loc1)
            z_copy(w, c).start()

        if takes:
            put(tq, w, c, jnp.where(first, in1, in0))
            t_copy(w, c).start()
        else:
            @pl.when(first)
            def _():
                put(tq, w, c, in1)
                t_copy(w, c).start()

        ins[w, b, part] = jnp.where(first, in0, in1)

    def grad(w, b):
        st = split((ins[w, b] * scl[1 - w, b][:, None, :]).reshape(rows, state))
        both = jnp.concatenate(st, axis=1)
        m = mm(both, hi[1 - w, b], 0, 0)
        gacc[w] += m[:state] + m[state:] + mm(st[0], lo[1 - w, b], 0, 0)
        return both

    def result(w, b, both):
        y = ys[w, b] + mm(both, proj[1 - w], 1, 1)
        skip = skp[b][:, 0:1][:, :, None]
        res_ref[w, hblock(b)] = (
            y.reshape(hb, width, tok) * fac[1 - w, b][:, None, :]
            + skip * inp[w, hblock(b)].astype(F32)
        ).astype(BF16)

    def p3(w, b):
        result(w, b, grad(w, b))

    def take(w, k):
        b = (1 - x) * GROUP + k

        def read():
            for i in range(cuts):
                t_copy(w, k * cuts + i).wait_recv()
                ins[w, b, cut(i)] = get(tr, w, k * cuts + i, piece)

        if w is late:
            read()
            return b

        none = edge & leads_early

        @pl.when(none)
        def _():
            ins[w, b] = jnp.zeros_like(ins[w, b])

        pl.when(jnp.logical_not(none))(read)
        return b

    def c_copy(w):
        return rcopy(gsc.at[w, 1 - core], grc.at[w], csem, (w,), me, mate)

    def y_copy(w, d, slot):
        return rcopy(hx.at[w, slot], hx.at[w, slot], ysem, (w, d), me, lax.rem(hd + 2 * d, nhead))

    def f_copy(w, slot):
        return rcopy(gfin.at[w, slot], gfin.at[w, slot], fsem, (w,), me, mate)

    def reduce_core(w):
        kept = seg_row == jnp.where(w == 0, prior, seg_last)
        g = gloc[w] + jnp.where(kept, gacc[w], 0.0)
        gsc[w, 0], gsc[w, 1] = g[:, :half], g[:, half:]
        c_copy(w).start()

    def reduce_rows(w):
        c_copy(w).wait_recv()
        v = gsc[w, core] + grc[w]
        top = jnp.max(jnp.abs(v), axis=0, keepdims=True)
        power = jnp.ceil(jnp.log2(jnp.maximum(top, 1e-30)))
        code = jnp.round(v * (jnp.exp2(-power) * 32000.0))
        hx[w, yy, :state] = code.astype(jnp.int32).astype(jnp.int16)
        hx[w, yy, state:] = (
            jnp.broadcast_to(power, (16, half)).astype(jnp.int32).astype(jnp.int16)
        )
        for d in range(1, ny):
            y_copy(w, d, yy).start()

    def reduce_end(w):
        for d in range(1, ny):
            y_copy(w, d, lax.rem(yy + ny - d, ny)).wait_recv()
        total = jnp.zeros((state, half), F32)
        for j in range(ny):
            power = hx[w, j, state:].astype(jnp.int32).astype(F32)[0:1]
            code = hx[w, j, :state].astype(jnp.int32).astype(F32)
            total = total + code * (jnp.exp2(power) * (1.0 / 32000.0))
        gfin[w, core] = total.T.astype(BF16)
        f_copy(w, core).start()

    @pl.loop(0, GROUP)
    def _(k):
        @pl.when(k == 0)
        def _():
            p_copy().wait_recv()

        @pl.when(edge)
        def _():
            handle(early, k, 0, True, False)

        p2_out(k)
        p2_mix(k)

    @pl.loop(0, GROUP)
    def _(k):
        @pl.when(jnp.logical_not(edge))
        def _():
            handle(early, k, 0, True, True)

        p2_grad(k)
        p2_mix(GROUP + k)

    @pl.loop(0, GROUP)
    def _(k):
        @pl.when(jnp.logical_not(edge))
        def _():
            for i in range(cuts):
                handle(late, k, i, True, True)

        p3(early, x * GROUP + k)

    mixed = split(jnp.where(same & (r_id >= c_id), macc[...], 0.0))
    keys, queries = key_ref[...], query_ref[...]
    gloc[0] = mm(keys, mixed[0], 0, 1) + mm(keys, mixed[1], 0, 1)
    gloc[1] = mm(queries, mixed[0], 0, 0) + mm(queries, mixed[1], 0, 0)

    @pl.loop(0, GROUP)
    def _(k):
        p3(early, take(early, k))

        @pl.when(edge)
        def _():
            for i in range(cuts):
                handle(late, k, i, False, True)

    reduce_core(early)

    @pl.loop(0, GROUP)
    def _(k):
        p3(late, x * GROUP + k)

    reduce_rows(early)

    @pl.loop(0, GROUP)
    def _(k):
        p3(late, take(late, k))

    reduce_core(late)
    reduce_end(early)
    reduce_rows(late)
    reduce_end(late)
    for w in range(2):
        f_copy(w, 1 - core).wait_recv()
    for j in range(2):
        gq_ref[j * half : (j + 1) * half] = gfin[0, j]
        gk_ref[j * half : (j + 1) * half] = gfin[1, j]

    p_copy().wait_send()
    for w in range(2):
        c_copy(w).wait_send()
        f_copy(w, core).wait_send()
        for d in range(1, ny):
            y_copy(w, d, yy).wait_send()

    @pl.loop(0, GROUP * cuts)
    def _(k):
        x_copy(early, k).wait_send()
        z_copy(early, k).wait_send()
        t_copy(late, k).wait_send()

        @pl.when(jnp.logical_not(edge) | leads_late)
        def _():
            x_copy(late, k).wait_send()

        @pl.when(jnp.logical_not(edge) | leads_early)
        def _():
            t_copy(early, k).wait_send()

        @pl.when(jnp.logical_not(edge))
        def _():
            z_copy(late, k).wait_send()


def store(res, gk, gq, out_ref, gs_ref, gk_ref, gq_ref, sems):
    pairs = ((res.at[0], out_ref), (res.at[1], gs_ref), (gk, gk_ref), (gq, gq_ref))
    copies = [pltpu.make_async_copy(a, b, sems.at[i]) for i, (a, b) in enumerate(pairs)]
    for copy in copies:
        copy.start()
    for copy in copies:
        copy.wait()


def solution(mesh):
    nseq, nhead = mesh.shape["seq"], mesh.shape["head"]

    def on_device(signal, step_raw, key_proj, query_proj, decay_log, skip_gain, lengths, cotangent):
        tok, heads, width = signal.shape
        state = key_proj.shape[1]
        blocks = 2 * GROUP
        hb = heads // blocks
        rows = hb * width
        half = tok // 2
        ny = nhead // 2
        dma = pltpu.SemaphoreType.DMA
        vmem = pltpu.VMEM
        cuts = 1
        chunks, hc = GROUP * cuts, hb // cuts
        st = (hb, width, state)
        scratch = (
            [pltpu.SMEM(lengths.shape, jnp.int32), vmem((heads, tok), BF16)]
            + [vmem((tok, state), BF16)] * 2
            + [vmem((1, heads), F32)] * 2
            + [vmem((2, heads, width, tok), BF16)]
            + [vmem((2, blocks, rows, tok), BF16)] * 2
            + [vmem((2, blocks, rows, tok), F32)]
            + [vmem((tok, tok), F32)]
            + [vmem((tok, tok), BF16)] * 4
            + [vmem((2, tok, 2 * state), BF16)]
            + [vmem((2, 2 * tok, state), BF16)]
            + [vmem((2, blocks, hb, tok), F32)]
            + [vmem((blocks, hb, state), F32)] * 2
            + [vmem((2, blocks, hb, state), F32)]
            + [vmem((blocks, hb, state), F32)]
            + [vmem((2, blocks) + st, F32)] * 2
            + [vmem((2, chunks, hc * width + 16, state), jnp.int16)] * 6
            + [vmem((2, state, tok), F32)] * 2
            + [vmem((2, 2, state, half), F32)]
            + [vmem((2, state, half), F32)]
            + [vmem((2, ny, state + 16, half), jnp.int16)]
            + [vmem((2, 2, half, state), BF16)]
            + [dma((6,)), dma((2, 2, 2)), dma((2,))]
            + [dma((2, 2, chunks))] * 3
            + [dma((2, 2)), dma((2, 2, ny)), dma((2, 2))]
        )
        turned = jax.ShapeDtypeStruct((heads, width, tok), BF16)
        grads = jax.ShapeDtypeStruct((tok, state), BF16)
        whole = pl.BlockSpec(memory_space=pltpu.VMEM)
        anywhere = pl.BlockSpec(memory_space=pl.ANY)
        res, gk, gq = pl.pallas_call(
            functools.partial(kernel, nseq, nhead),
            out_shape=(
                vmem((2, heads, width, tok), BF16), vmem((tok, state), BF16), vmem((tok, state), BF16)
            ),
            in_specs=[anywhere] * 8,
            out_specs=(whole,) * 3,
            scratch_shapes=scratch,
            compiler_params=pltpu.CompilerParams(
                collective_id=0, has_side_effects=True, vmem_limit_bytes=58 << 20
            ),
        )(
            lengths,
            jnp.transpose(signal, (1, 2, 0)),
            jnp.transpose(cotangent, (1, 2, 0)),
            step_raw.T,
            key_proj,
            query_proj,
            decay_log[None, :],
            skip_gain[None, :],
        )
        out, gs, gk, gq = pl.pallas_call(
            store,
            out_shape=(turned, turned, grads, grads),
            in_specs=[whole] * 3,
            out_specs=(anywhere,) * 4,
            scratch_shapes=[dma((4,))],
            compiler_params=pltpu.CompilerParams(vmem_limit_bytes=2 << 20),
        )(*(pltpu.with_memory_space_constraint(v, pltpu.VMEM) for v in (res, gk, gq)))
        return jnp.transpose(out, (2, 0, 1)), jnp.transpose(gs, (2, 0, 1)), gk, gq

    in_specs = (
        P("seq", "head", None),
        P("seq", "head"),
        P("seq", None),
        P("seq", None),
        P("head"),
        P("head"),
        P(),
        P("seq", "head", None),
    )
    out_specs = (P("seq", "head", None), P("seq", "head", None), P("seq", None), P("seq", None))
    return jax.shard_map(
        on_device, mesh=mesh, in_specs=in_specs, out_specs=out_specs, check_vma=False
    )
```

```python
import functools

import jax
import jax.numpy as jnp
from jax import lax
from jax.experimental import pallas as pl
from jax.experimental.pallas import tpu as pltpu
from jax.sharding import PartitionSpec as P

MESH = pl.DeviceIdType.MESH
F32 = jnp.float32
BF16 = jnp.bfloat16
GROUP = 4


def mm(a, b, ca=1, cb=0):
    return lax.dot_general(a, b, (((ca,), (cb,)), ((), ())), preferred_element_type=F32)


def split(a):
    hi = a.astype(BF16)
    return hi, (a - hi.astype(F32)).astype(BF16)


def mm3(a, b, ca=1, cb=0):
    return mm(a[0], b[0], ca, cb) + mm(a[0], b[1], ca, cb) + mm(a[1], b[0], ca, cb)


def put(ref, w, c, v):
    heads, width, state = v.shape
    top = jnp.max(jnp.abs(v), axis=1)
    power = jnp.ceil(jnp.log2(jnp.maximum(top, 1e-30)))
    code = jnp.round(v * (jnp.exp2(-power) * 32000.0)[:, None, :])
    ref[w, c, : heads * width] = code.reshape(heads * width, state).astype(jnp.int32).astype(jnp.int16)
    pad = jnp.concatenate([power, jnp.zeros((16 - heads, state), F32)], axis=0)
    ref[w, c, heads * width :] = pad.astype(jnp.int32).astype(jnp.int16)


def get(ref, w, c, shape):
    heads, width, state = shape
    power = ref[w, c, heads * width :].astype(jnp.int32).astype(F32)[:heads]
    code = ref[w, c, : heads * width].astype(jnp.int32).astype(F32).reshape(shape)
    return code * (jnp.exp2(power) * (1.0 / 32000.0))[:, None, :]


def kernel(
    nseq, nhead, len_in, sig, cot, step_in, key_in, query_in, dl_in, sk_in,
    res_ref, gk_ref, gq_ref,
    len_ref, step_ref, key_ref, query_ref, dl_ref, sk_ref, inp, hi, lo, ys, macc, gh, gl, gth, gtl, proj, tall, fac, pas, pasr, scl, skp, loc, ins,
    xq, xr, zq, zr, tq, tr, gacc, gloc, gsc, grc, hx, gfin,
    ssem, isem, psem, xsem, zsem, tsem, csem, ysem, fsem,
):
    _, heads, width, tok = inp.shape
    state = key_ref.shape[1]
    blocks = 2 * GROUP
    hb = heads // blocks
    rows = hb * width
    cuts = 1
    hc = hb // cuts
    piece = (hc, width, state)
    half = tok // 2
    ny = nhead // 2
    me, hd = lax.axis_index("seq"), lax.axis_index("head")
    x, z = lax.rem(me, 2), me // 2
    yy, core = hd // 2, lax.rem(hd, 2)
    nz = nseq // 2
    partner = me + 1 - 2 * x
    mate = hd + 1 - 2 * core
    early = jnp.where(z < nz // 2, 0, 1)
    late = 1 - early

    barrier = pltpu.get_barrier_semaphore()

    def greet(seq, head):
        pl.semaphore_signal(barrier, inc=1, device_id=(seq, head), device_id_type=MESH)

    greet(partner, hd)

    @pl.when(z > 0)
    def _():
        greet(me - 2, hd)

    @pl.when(z < nz - 1)
    def _():
        greet(me + 2, hd)

    greet(me, mate)
    for d in range(1, ny):
        greet(me, lax.rem(hd + 2 * d, nhead))

    small = [
        pltpu.make_async_copy(a, b, ssem.at[n])
        for n, (a, b) in enumerate(
            (
                (step_in, step_ref), (dl_in, dl_ref), (len_in, len_ref), (key_in, key_ref),
                (query_in, query_ref), (sk_in, sk_ref),
            )
        )
    ]
    for copy in small:
        copy.start()

    sides = (1 - x, x)

    def hblock(b):
        return pl.ds(b * hb, hb)

    def in_copy(src, w, j, k, size):
        part = pl.ds((sides[j] * GROUP + k) * hb, size * hb)
        return pltpu.make_async_copy(src.at[part], inp.at[w, part], isem.at[w, j, 1 if k else 0])

    def fetch(w, j, k, size):
        @pl.when(w == 0)
        def _():
            in_copy(sig, 0, j, k, size).start()

        @pl.when(w == 1)
        def _():
            in_copy(cot, 1, j, k, size).start()

    fetch(early, 0, 0, 1)

    def rcopy(src, dst, sems, index, seq, head=None):
        return pltpu.make_async_remote_copy(
            src_ref=src, dst_ref=dst, send_sem=sems.at[(0,) + index], recv_sem=sems.at[(1,) + index],
            device_id=(seq, hd if head is None else head), device_id_type=MESH,
        )

    def p_copy():
        return rcopy(pas, pasr, psem, (), partner)

    def x_copy(w, c):
        return rcopy(xq.at[w, c], xr.at[w, c], xsem, (w, c), partner)

    def z_copy(w, c):
        return rcopy(zq.at[w, c], zr.at[w, c], zsem, (w, c), me + 2 - 4 * w)

    def t_copy(w, c):
        return rcopy(tq.at[w, c], tr.at[w, c], tsem, (w, c), partner)

    def cut(i):
        return slice(i * hc, (i + 1) * hc)

    rank = jnp.where(early == 0, z, nz - 1 - z)
    edge = rank == 0
    leads_early, leads_late = x == early, x == late

    for copy in small:
        copy.wait()

    start = me * tok
    end, ends = jnp.int32(0), []
    for k in range(len_ref.shape[0]):
        end = end + len_ref[k]
        ends.append(end)

    def segment(places):
        total = jnp.zeros_like(places)
        for value in ends:
            total = total + jnp.where(places >= value, 1, 0)
        return total

    seg_last = segment(start + tok - 1)
    prior = jnp.where(start > 0, segment(start - 1), -1)
    begin, stop = jnp.int32(0), jnp.where(start > 0, jnp.int32(nseq * tok), 0)
    for value in reversed(ends):
        stop = jnp.where((value >= start) & (start > 0), value, stop)
    for value in ends:
        begin = jnp.where(value <= start + tok - 1, value, begin)
    upper = jnp.where(
        lax.broadcasted_iota(jnp.int32, (half, half), 0)
        <= lax.broadcasted_iota(jnp.int32, (half, half), 1),
        1.0,
        0.0,
    ).astype(BF16)

    raw = step_ref[...].astype(F32)
    size = jnp.maximum(raw, 0.0) + jnp.log1p(jnp.exp(-jnp.abs(raw)))
    eye = lax.broadcasted_iota(jnp.int32, (heads, heads), 0) == lax.broadcasted_iota(
        jnp.int32, (heads, heads), 1
    )
    column = lambda ref: jnp.sum(jnp.where(eye, ref[...], 0.0), axis=1, keepdims=True)
    logdec = size * (-jnp.exp(column(dl_ref)))
    one = logdec.astype(BF16)
    rest = logdec - one.astype(F32)
    two, three = split(rest)
    parts = [p[:, j * half : (j + 1) * half] for j in range(2) for p in (one, two, three)]
    sums = mm(jnp.concatenate(parts, axis=0), upper)
    sums = [sums[i * heads : (i + 1) * heads] for i in range(6)]
    cum0 = sums[2] + sums[1] + sums[0]
    mid = cum0[:, half - 1 : half]
    cum = jnp.concatenate([cum0, sums[5] + sums[4] + sums[3] + mid], axis=1)
    final = cum[:, tok - 1 : tok]
    e = jnp.exp(cum - mid)
    f = size * jnp.exp(mid - cum)
    lanes = (heads, state)
    passing = jnp.broadcast_to(jnp.where(seg_last == prior, jnp.exp(final), 0.0), lanes)
    to_last = jnp.broadcast_to(jnp.exp(final - mid), lanes)
    to_mid = jnp.broadcast_to(jnp.exp(mid), lanes)
    skips = jnp.broadcast_to(column(sk_ref), lanes)
    for b in range(blocks):
        part = slice(b * hb, (b + 1) * hb)
        fac[0, b], fac[1, b] = f[part], e[part]
        scl[0, b], scl[1, b] = to_last[part], to_mid[part]
        pas[b], skp[b] = passing[part], skips[part]

    place = start + lax.broadcasted_iota(jnp.int32, (tok, state), 0)
    km = jnp.where(place >= begin, key_ref[...].astype(F32), 0.0).astype(BF16)
    qm = jnp.where(place < stop, query_ref[...].astype(F32), 0.0).astype(BF16)
    for j in range(2):
        proj[0, :, j * state : (j + 1) * state] = km
        proj[1, :, j * state : (j + 1) * state] = qm
        tall[0, j * tok : (j + 1) * tok] = km
        tall[1, j * tok : (j + 1) * tok] = qm

    fetch(early, 0, 1, GROUP - 1)
    fetch(late, 0, 0, GROUP)
    fetch(early, 1, 0, GROUP)
    fetch(late, 1, 0, GROUP)

    pl.semaphore_wait(
        barrier, 1 + ny + jnp.where(z > 0, 1, 0) + jnp.where(z < nz - 1, 1, 0)
    )
    p_copy().start()

    def p1(w, b):
        t = inp[w, hblock(b)].astype(F32) * fac[w, b][:, None, :]
        top, low = split(t.reshape(rows, tok))
        hi[w, b], lo[w, b] = top, low
        both = jnp.concatenate([top, low], axis=1)
        return mm(both, tall[w]).reshape(hb, width, state) * scl[w, b][:, None, :]

    in_copy(sig, early, 0, 0, 1).wait()
    for w in (early, late):
        if w is late:
            in_copy(sig, late, 0, 0, GROUP).wait()

        @pl.loop(0, GROUP)
        def _(k):
            if w is early:
                @pl.when(k == 1)
                def _():
                    in_copy(sig, early, 0, 1, GROUP - 1).wait()

            value = p1(w, (1 - x) * GROUP + k)
            for i in range(cuts):
                c = k * cuts + i
                put(xq, w, c, value[cut(i)])
                if w is early:
                    x_copy(w, c).start()
                else:
                    @pl.when(jnp.logical_not(edge) | leads_late)
                    def _():
                        x_copy(w, c).start()

    for w in (early, late):
        in_copy(sig, w, 1, 0, GROUP).wait()

        @pl.loop(0, GROUP)
        def _(k):
            b = x * GROUP + k
            loc[w, b] = p1(w, b)

    r_id = lax.broadcasted_iota(jnp.int32, (tok, tok), 0)
    c_id = lax.broadcasted_iota(jnp.int32, (tok, tok), 1)
    seg_col = segment(start + lax.broadcasted_iota(jnp.int32, (tok, 1), 0))
    seg_row = segment(start + lax.broadcasted_iota(jnp.int32, (1, tok), 1))
    keys, queries = key_ref[...], query_ref[...]
    same = seg_col == seg_row
    gram = jnp.where(same & (r_id >= c_id), mm(queries, keys, 1, 1), 0.0)
    gh[...], gl[...] = split(gram)
    gram_t = jnp.where(same & (r_id <= c_id), mm(keys, queries, 1, 1), 0.0)
    gth[...], gtl[...] = split(gram_t)
    macc[...] = jnp.zeros_like(macc)
    gacc[...] = jnp.zeros_like(gacc)

    def pair(ref, w, k):
        return ref[w, pl.ds(2 * k, 2)].reshape(2 * rows, tok)

    def p2_out(k):
        bb = (pair(hi, 0, k), pair(lo, 0, k))
        b0 = (bb[0][:, :half], bb[1][:, :half])
        left = mm3(b0, (gth[:half, :half], gtl[:half, :half]))
        ys[0, pl.ds(2 * k, 2), :, :half] = left.reshape(2, rows, half)
        right = mm3(bb, (gth[:, half:], gtl[:, half:]))
        ys[0, pl.ds(2 * k, 2), :, half:] = right.reshape(2, rows, half)

    def p2_grad(k):
        aa = (pair(hi, 1, k), pair(lo, 1, k))
        a1 = (aa[0][:, half:], aa[1][:, half:])
        right = mm3(a1, (gh[half:, half:], gl[half:, half:]))
        ys[1, pl.ds(2 * k, 2), :, half:] = right.reshape(2, rows, half)
        left = mm3(aa, (gh[:, :half], gl[:, :half]))
        ys[1, pl.ds(2 * k, 2), :, :half] = left.reshape(2, rows, half)

    def p2_mix(b):
        bb = (hi[0, b], lo[0, b])
        aa = (hi[1, b], lo[1, b])
        b0 = (bb[0][:, :half], bb[1][:, :half])
        a0 = (aa[0][:, :half], aa[1][:, :half])
        a1 = (aa[0][:, half:], aa[1][:, half:])
        macc[:half, :half] += mm3(a0, b0, 0, 0)
        macc[half:, :] += mm3(a1, bb, 0, 0)

    def handle(w, k, i, sends, takes):
        b, c, part = x * GROUP + k, k * cuts + i, cut(i)
        first = x == w
        if sends:
            x_copy(w, c).wait_recv()
        else:
            @pl.when(jnp.logical_not(first))
            def _():
                x_copy(w, c).wait_recv()

        if takes:
            z_copy(w, c).wait_recv()

        own, other = pas[b, part][:, None, :], pasr[b, part][:, None, :]
        mine, theirs = loc[w, b, part], get(xr, w, c, piece)
        pass0, pass1 = jnp.where(first, own, other), jnp.where(first, other, own)
        loc0, loc1 = jnp.where(first, mine, theirs), jnp.where(first, theirs, mine)
        in0 = get(zr, w, c, piece) if takes else jnp.zeros_like(mine)
        in1 = pass0 * in0 + loc0
        if sends:
            put(zq, w, c, pass1 * in1 + loc1)
            z_copy(w, c).start()

        if takes:
            put(tq, w, c, jnp.where(first, in1, in0))
            t_copy(w, c).start()
        else:
            @pl.when(first)
            def _():
                put(tq, w, c, in1)
                t_copy(w, c).start()

        ins[w, b, part] = jnp.where(first, in0, in1)

    def grad(w, b):
        st = split((ins[w, b] * scl[1 - w, b][:, None, :]).reshape(rows, state))
        both = jnp.concatenate(st, axis=1)
        m = mm(both, hi[1 - w, b], 0, 0)
        gacc[w] += m[:state] + m[state:] + mm(st[0], lo[1 - w, b], 0, 0)
        return both

    def result(w, b, both):
        y = ys[w, b] + mm(both, proj[1 - w], 1, 1)
        skip = skp[b][:, 0:1][:, :, None]
        res_ref[w, hblock(b)] = (
            y.reshape(hb, width, tok) * fac[1 - w, b][:, None, :]
            + skip * inp[w, hblock(b)].astype(F32)
        ).astype(BF16)

    def p3(w, b):
        result(w, b, grad(w, b))

    def take(w, k):
        b = (1 - x) * GROUP + k

        def read():
            for i in range(cuts):
                t_copy(w, k * cuts + i).wait_recv()
                ins[w, b, cut(i)] = get(tr, w, k * cuts + i, piece)

        if w is late:
            read()
            return b

        none = edge & leads_early

        @pl.when(none)
        def _():
            ins[w, b] = jnp.zeros_like(ins[w, b])

        pl.when(jnp.logical_not(none))(read)
        return b

    def c_copy(w):
        return rcopy(gsc.at[w, 1 - core], grc.at[w], csem, (w,), me, mate)

    def y_copy(w, d, slot):
        return rcopy(hx.at[w, slot], hx.at[w, slot], ysem, (w, d), me, lax.rem(hd + 2 * d, nhead))

    def f_copy(w, slot):
        return rcopy(gfin.at[w, slot], gfin.at[w, slot], fsem, (w,), me, mate)

    def reduce_core(w):
        kept = seg_row == jnp.where(w == 0, prior, seg_last)
        g = gloc[w] + jnp.where(kept, gacc[w], 0.0)
        gsc[w, 0], gsc[w, 1] = g[:, :half], g[:, half:]
        c_copy(w).start()

    def reduce_rows(w):
        c_copy(w).wait_recv()
        v = gsc[w, core] + grc[w]
        top = jnp.max(jnp.abs(v), axis=0, keepdims=True)
        power = jnp.ceil(jnp.log2(jnp.maximum(top, 1e-30)))
        code = jnp.round(v * (jnp.exp2(-power) * 32000.0))
        hx[w, yy, :state] = code.astype(jnp.int32).astype(jnp.int16)
        hx[w, yy, state:] = (
            jnp.broadcast_to(power, (16, half)).astype(jnp.int32).astype(jnp.int16)
        )
        for d in range(1, ny):
            y_copy(w, d, yy).start()

    def reduce_end(w):
        for d in range(1, ny):
            y_copy(w, d, lax.rem(yy + ny - d, ny)).wait_recv()
        total = jnp.zeros((state, half), F32)
        for j in range(ny):
            power = hx[w, j, state:].astype(jnp.int32).astype(F32)[0:1]
            code = hx[w, j, :state].astype(jnp.int32).astype(F32)
            total = total + code * (jnp.exp2(power) * (1.0 / 32000.0))
        gfin[w, core] = total.T.astype(BF16)
        f_copy(w, core).start()

    @pl.loop(0, GROUP)
    def _(k):
        @pl.when(k == 0)
        def _():
            p_copy().wait_recv()

        @pl.when(edge)
        def _():
            handle(early, k, 0, True, False)

        p2_out(k)
        p2_mix(k)

    @pl.loop(0, GROUP)
    def _(k):
        @pl.when(jnp.logical_not(edge))
        def _():
            handle(early, k, 0, True, True)

        p2_grad(k)
        p2_mix(GROUP + k)

    @pl.loop(0, GROUP)
    def _(k):
        @pl.when(jnp.logical_not(edge))
        def _():
            for i in range(cuts):
                handle(late, k, i, True, True)

        p3(early, x * GROUP + k)

    mixed = split(jnp.where(same & (r_id >= c_id), macc[...], 0.0))
    keys, queries = key_ref[...], query_ref[...]
    gloc[0] = mm(keys, mixed[0], 0, 1) + mm(keys, mixed[1], 0, 1)
    gloc[1] = mm(queries, mixed[0], 0, 0) + mm(queries, mixed[1], 0, 0)

    @pl.loop(0, GROUP)
    def _(k):
        p3(early, take(early, k))

    reduce_core(early)

    @pl.loop(0, GROUP)
    def _(k):
        @pl.when(edge)
        def _():
            for i in range(cuts):
                handle(late, k, i, False, True)

        p3(late, x * GROUP + k)

        @pl.when(k == 1)
        def _():
            reduce_rows(early)

    @pl.loop(0, GROUP)
    def _(k):
        p3(late, take(late, k))

    reduce_core(late)
    reduce_rows(late)

    p_copy().wait_send()
    @pl.loop(0, GROUP * cuts)
    def _(k):
        x_copy(early, k).wait_send()
        z_copy(early, k).wait_send()
        t_copy(late, k).wait_send()

        @pl.when(jnp.logical_not(edge) | leads_late)
        def _():
            x_copy(late, k).wait_send()

        @pl.when(jnp.logical_not(edge) | leads_early)
        def _():
            t_copy(early, k).wait_send()

        @pl.when(jnp.logical_not(edge))
        def _():
            z_copy(late, k).wait_send()

    reduce_end(early)
    reduce_end(late)
    for w in range(2):
        f_copy(w, 1 - core).wait_recv()
    for j in range(2):
        gq_ref[j * half : (j + 1) * half] = gfin[0, j]
        gk_ref[j * half : (j + 1) * half] = gfin[1, j]

    for w in range(2):
        c_copy(w).wait_send()
        f_copy(w, core).wait_send()
        for d in range(1, ny):
            y_copy(w, d, yy).wait_send()


def store(res, gk, gq, out_ref, gs_ref, gk_ref, gq_ref, sems):
    pairs = ((res.at[0], out_ref), (res.at[1], gs_ref), (gk, gk_ref), (gq, gq_ref))
    copies = [pltpu.make_async_copy(a, b, sems.at[i]) for i, (a, b) in enumerate(pairs)]
    for copy in copies:
        copy.start()
    for copy in copies:
        copy.wait()


def solution(mesh):
    nseq, nhead = mesh.shape["seq"], mesh.shape["head"]

    def on_device(signal, step_raw, key_proj, query_proj, decay_log, skip_gain, lengths, cotangent):
        tok, heads, width = signal.shape
        state = key_proj.shape[1]
        blocks = 2 * GROUP
        hb = heads // blocks
        rows = hb * width
        half = tok // 2
        ny = nhead // 2
        dma = pltpu.SemaphoreType.DMA
        vmem = pltpu.VMEM
        cuts = 1
        chunks, hc = GROUP * cuts, hb // cuts
        st = (hb, width, state)
        scratch = (
            [pltpu.SMEM(lengths.shape, jnp.int32), vmem((heads, tok), BF16)]
            + [vmem((tok, state), BF16)] * 2
            + [vmem((1, heads), F32)] * 2
            + [vmem((2, heads, width, tok), BF16)]
            + [vmem((2, blocks, rows, tok), BF16)] * 2
            + [vmem((2, blocks, rows, tok), F32)]
            + [vmem((tok, tok), F32)]
            + [vmem((tok, tok), BF16)] * 4
            + [vmem((2, tok, 2 * state), BF16)]
            + [vmem((2, 2 * tok, state), BF16)]
            + [vmem((2, blocks, hb, tok), F32)]
            + [vmem((blocks, hb, state), F32)] * 2
            + [vmem((2, blocks, hb, state), F32)]
            + [vmem((blocks, hb, state), F32)]
            + [vmem((2, blocks) + st, F32)] * 2
            + [vmem((2, chunks, hc * width + 16, state), jnp.int16)] * 6
            + [vmem((2, state, tok), F32)] * 2
            + [vmem((2, 2, state, half), F32)]
            + [vmem((2, state, half), F32)]
            + [vmem((2, ny, state + 16, half), jnp.int16)]
            + [vmem((2, 2, half, state), BF16)]
            + [dma((6,)), dma((2, 2, 2)), dma((2,))]
            + [dma((2, 2, chunks))] * 3
            + [dma((2, 2)), dma((2, 2, ny)), dma((2, 2))]
        )
        turned = jax.ShapeDtypeStruct((heads, width, tok), BF16)
        grads = jax.ShapeDtypeStruct((tok, state), BF16)
        whole = pl.BlockSpec(memory_space=pltpu.VMEM)
        anywhere = pl.BlockSpec(memory_space=pl.ANY)
        res, gk, gq = pl.pallas_call(
            functools.partial(kernel, nseq, nhead),
            out_shape=(
                vmem((2, heads, width, tok), BF16), vmem((tok, state), BF16), vmem((tok, state), BF16)
            ),
            in_specs=[anywhere] * 8,
            out_specs=(whole,) * 3,
            scratch_shapes=scratch,
            compiler_params=pltpu.CompilerParams(
                collective_id=0, has_side_effects=True, vmem_limit_bytes=58 << 20
            ),
        )(
            lengths,
            jnp.transpose(signal, (1, 2, 0)),
            jnp.transpose(cotangent, (1, 2, 0)),
            step_raw.T,
            key_proj,
            query_proj,
            decay_log[None, :],
            skip_gain[None, :],
        )
        out, gs, gk, gq = pl.pallas_call(
            store,
            out_shape=(turned, turned, grads, grads),
            in_specs=[whole] * 3,
            out_specs=(anywhere,) * 4,
            scratch_shapes=[dma((4,))],
            compiler_params=pltpu.CompilerParams(vmem_limit_bytes=2 << 20),
        )(*(pltpu.with_memory_space_constraint(v, pltpu.VMEM) for v in (res, gk, gq)))
        return jnp.transpose(out, (2, 0, 1)), jnp.transpose(gs, (2, 0, 1)), gk, gq

    in_specs = (
        P("seq", "head", None),
        P("seq", "head"),
        P("seq", None),
        P("seq", None),
        P("head"),
        P("head"),
        P(),
        P("seq", "head", None),
    )
    out_specs = (P("seq", "head", None), P("seq", "head", None), P("seq", None), P("seq", None))
    return jax.shard_map(
        on_device, mesh=mesh, in_specs=in_specs, out_specs=out_specs, check_vma=False
    )
```

```python
import functools

import jax
import jax.numpy as jnp
from jax import lax
from jax.experimental import pallas as pl
from jax.experimental.pallas import tpu as pltpu
from jax.sharding import PartitionSpec as P

MESH = pl.DeviceIdType.MESH
F32 = jnp.float32
BF16 = jnp.bfloat16
GROUP = 4


def mm(a, b, ca=1, cb=0):
    return lax.dot_general(a, b, (((ca,), (cb,)), ((), ())), preferred_element_type=F32)


def split(a):
    hi = a.astype(BF16)
    return hi, (a - hi.astype(F32)).astype(BF16)


def mm3(a, b, ca=1, cb=0):
    return mm(a[0], b[0], ca, cb) + mm(a[0], b[1], ca, cb) + mm(a[1], b[0], ca, cb)


def put(ref, w, c, v):
    heads, width, state = v.shape
    top = jnp.max(jnp.abs(v), axis=1)
    power = jnp.ceil(jnp.log2(jnp.maximum(top, 1e-30)))
    code = jnp.round(v * (jnp.exp2(-power) * 32000.0)[:, None, :])
    ref[w, c, : heads * width] = code.reshape(heads * width, state).astype(jnp.int32).astype(jnp.int16)
    pad = jnp.concatenate([power, jnp.zeros((16 - heads, state), F32)], axis=0)
    ref[w, c, heads * width :] = pad.astype(jnp.int32).astype(jnp.int16)


def get(ref, w, c, shape):
    heads, width, state = shape
    power = ref[w, c, heads * width :].astype(jnp.int32).astype(F32)[:heads]
    code = ref[w, c, : heads * width].astype(jnp.int32).astype(F32).reshape(shape)
    return code * (jnp.exp2(power) * (1.0 / 32000.0))[:, None, :]


def kernel(
    nseq, nhead, len_in, sig, cot, step_in, key_in, query_in, dl_in, sk_in,
    res_ref, gk_ref, gq_ref,
    len_ref, step_ref, key_ref, query_ref, dl_ref, sk_ref, inp, hi, lo, ys, macc, gh, gl, gth, gtl, proj, tall, fac, pas, pasr, scl, skp, loc, ins,
    xq, xr, zq, zr, tq, tr, pairs, gacc, gloc, gsc, grc, hx, gfin,
    ssem, isem, psem, xsem, zsem, tsem, csem, ysem, fsem,
):
    _, heads, width, tok = inp.shape
    state = key_ref.shape[1]
    blocks = 2 * GROUP
    hb = heads // blocks
    rows = hb * width
    cuts = 1
    hc = hb // cuts
    piece = (hc, width, state)
    half = tok // 2
    ny = nhead // 2
    me, hd = lax.axis_index("seq"), lax.axis_index("head")
    x, z = lax.rem(me, 2), me // 2
    yy, core = hd // 2, lax.rem(hd, 2)
    nz = nseq // 2
    partner = me + 1 - 2 * x
    mate = hd + 1 - 2 * core
    early = jnp.where(z < nz // 2, 0, 1)
    late = 1 - early

    barrier = pltpu.get_barrier_semaphore()

    def greet(seq, head):
        pl.semaphore_signal(barrier, inc=1, device_id=(seq, head), device_id_type=MESH)

    greet(partner, hd)

    @pl.when(z > 0)
    def _():
        greet(me - 2, hd)

    @pl.when(z < nz - 1)
    def _():
        greet(me + 2, hd)

    greet(me, mate)
    for d in range(1, ny):
        greet(me, lax.rem(hd + 2 * d, nhead))

    small = [
        pltpu.make_async_copy(a, b, ssem.at[n])
        for n, (a, b) in enumerate(
            (
                (step_in, step_ref), (dl_in, dl_ref), (len_in, len_ref), (key_in, key_ref),
                (query_in, query_ref), (sk_in, sk_ref),
            )
        )
    ]
    for copy in small:
        copy.start()

    sides = (1 - x, x)

    def hblock(b):
        return pl.ds(b * hb, hb)

    def in_copy(src, w, j, k, size):
        part = pl.ds((sides[j] * GROUP + k) * hb, size * hb)
        return pltpu.make_async_copy(src.at[part], inp.at[w, part], isem.at[w, j, 1 if k else 0])

    def fetch(w, j, k, size):
        @pl.when(w == 0)
        def _():
            in_copy(sig, 0, j, k, size).start()

        @pl.when(w == 1)
        def _():
            in_copy(cot, 1, j, k, size).start()

    fetch(early, 0, 0, 1)

    def rcopy(src, dst, sems, index, seq, head=None):
        return pltpu.make_async_remote_copy(
            src_ref=src, dst_ref=dst, send_sem=sems.at[(0,) + index], recv_sem=sems.at[(1,) + index],
            device_id=(seq, hd if head is None else head), device_id_type=MESH,
        )

    def p_copy():
        return rcopy(pas, pasr, psem, (), partner)

    def x_copy(w, c):
        return rcopy(xq.at[w, c], xr.at[w, c], xsem, (w, c), partner)

    def z_copy(w, c):
        return rcopy(zq.at[w, c], zr.at[w, c], zsem, (w, c), me + 2 - 4 * w)

    def t_copy(w, c):
        return rcopy(tq.at[w, c], tr.at[w, c], tsem, (w, c), partner)

    def cut(i):
        return slice(i * hc, (i + 1) * hc)

    rank = jnp.where(early == 0, z, nz - 1 - z)
    edge = rank == 0
    leads_early, leads_late = x == early, x == late

    for copy in small:
        copy.wait()

    start = me * tok
    end, ends = jnp.int32(0), []
    for k in range(len_ref.shape[0]):
        end = end + len_ref[k]
        ends.append(end)

    def segment(places):
        total = jnp.zeros_like(places)
        for value in ends:
            total = total + jnp.where(places >= value, 1, 0)
        return total

    seg_last = segment(start + tok - 1)
    prior = jnp.where(start > 0, segment(start - 1), -1)
    begin, stop = jnp.int32(0), jnp.where(start > 0, jnp.int32(nseq * tok), 0)
    for value in reversed(ends):
        stop = jnp.where((value >= start) & (start > 0), value, stop)
    for value in ends:
        begin = jnp.where(value <= start + tok - 1, value, begin)
    upper = jnp.where(
        lax.broadcasted_iota(jnp.int32, (half, half), 0)
        <= lax.broadcasted_iota(jnp.int32, (half, half), 1),
        1.0,
        0.0,
    ).astype(BF16)

    raw = step_ref[...].astype(F32)
    size = jnp.maximum(raw, 0.0) + jnp.log1p(jnp.exp(-jnp.abs(raw)))
    eye = lax.broadcasted_iota(jnp.int32, (heads, heads), 0) == lax.broadcasted_iota(
        jnp.int32, (heads, heads), 1
    )
    column = lambda ref: jnp.sum(jnp.where(eye, ref[...], 0.0), axis=1, keepdims=True)
    logdec = size * (-jnp.exp(column(dl_ref)))
    one = logdec.astype(BF16)
    rest = logdec - one.astype(F32)
    two, three = split(rest)
    parts = [p[:, j * half : (j + 1) * half] for j in range(2) for p in (one, two, three)]
    sums = mm(jnp.concatenate(parts, axis=0), upper)
    sums = [sums[i * heads : (i + 1) * heads] for i in range(6)]
    cum0 = sums[2] + sums[1] + sums[0]
    mid = cum0[:, half - 1 : half]
    cum = jnp.concatenate([cum0, sums[5] + sums[4] + sums[3] + mid], axis=1)
    final = cum[:, tok - 1 : tok]
    e = jnp.exp(cum - mid)
    f = size * jnp.exp(mid - cum)
    lanes = (heads, state)
    passing = jnp.broadcast_to(jnp.where(seg_last == prior, jnp.exp(final), 0.0), lanes)
    to_last = jnp.broadcast_to(jnp.exp(final - mid), lanes)
    to_mid = jnp.broadcast_to(jnp.exp(mid), lanes)
    skips = jnp.broadcast_to(column(sk_ref), lanes)
    for b in range(blocks):
        part = slice(b * hb, (b + 1) * hb)
        fac[0, b], fac[1, b] = f[part], e[part]
        scl[0, b], scl[1, b] = to_last[part], to_mid[part]
        pas[b], skp[b] = passing[part], skips[part]

    place = start + lax.broadcasted_iota(jnp.int32, (tok, state), 0)
    km = jnp.where(place >= begin, key_ref[...].astype(F32), 0.0).astype(BF16)
    qm = jnp.where(place < stop, query_ref[...].astype(F32), 0.0).astype(BF16)
    for j in range(2):
        proj[0, :, j * state : (j + 1) * state] = km
        proj[1, :, j * state : (j + 1) * state] = qm
        tall[0, j * tok : (j + 1) * tok] = km
        tall[1, j * tok : (j + 1) * tok] = qm

    fetch(early, 0, 1, GROUP - 1)
    fetch(late, 0, 0, GROUP)
    fetch(early, 1, 0, GROUP)
    fetch(late, 1, 0, GROUP)

    pl.semaphore_wait(
        barrier, 1 + ny + jnp.where(z > 0, 1, 0) + jnp.where(z < nz - 1, 1, 0)
    )
    p_copy().start()

    def p1(w, b):
        t = inp[w, hblock(b)].astype(F32) * fac[w, b][:, None, :]
        top, low = split(t.reshape(rows, tok))
        hi[w, b], lo[w, b] = top, low
        both = jnp.concatenate([top, low], axis=1)
        return mm(both, tall[w]).reshape(hb, width, state) * scl[w, b][:, None, :]

    in_copy(sig, early, 0, 0, 1).wait()
    for w in (early, late):
        if w is late:
            in_copy(sig, late, 0, 0, GROUP).wait()

        @pl.loop(0, GROUP)
        def _(k):
            if w is early:
                @pl.when(k == 1)
                def _():
                    in_copy(sig, early, 0, 1, GROUP - 1).wait()

            value = p1(w, (1 - x) * GROUP + k)
            for i in range(cuts):
                c = k * cuts + i
                put(xq, w, c, value[cut(i)])
                if w is early:
                    x_copy(w, c).start()
                else:
                    @pl.when(jnp.logical_not(edge) | leads_late)
                    def _():
                        x_copy(w, c).start()

    for w in (early, late):
        in_copy(sig, w, 1, 0, GROUP).wait()

        @pl.loop(0, GROUP)
        def _(k):
            b = x * GROUP + k
            loc[w, b] = p1(w, b)

    r_id = lax.broadcasted_iota(jnp.int32, (tok, tok), 0)
    c_id = lax.broadcasted_iota(jnp.int32, (tok, tok), 1)
    seg_col = segment(start + lax.broadcasted_iota(jnp.int32, (tok, 1), 0))
    seg_row = segment(start + lax.broadcasted_iota(jnp.int32, (1, tok), 1))
    keys, queries = key_ref[...], query_ref[...]
    same = seg_col == seg_row
    gram = jnp.where(same & (r_id >= c_id), mm(queries, keys, 1, 1), 0.0)
    gh[...], gl[...] = split(gram)
    gram_t = jnp.where(same & (r_id <= c_id), mm(keys, queries, 1, 1), 0.0)
    gth[...], gtl[...] = split(gram_t)
    macc[...] = jnp.zeros_like(macc)
    gacc[...] = jnp.zeros_like(gacc)

    def pair(ref, w, k):
        return ref[w, pl.ds(2 * k, 2)].reshape(2 * rows, tok)

    def p2_out(k):
        bb = (pair(hi, 0, k), pair(lo, 0, k))
        b0 = (bb[0][:, :half], bb[1][:, :half])
        left = mm3(b0, (gth[:half, :half], gtl[:half, :half]))
        ys[0, pl.ds(2 * k, 2), :, :half] = left.reshape(2, rows, half)
        right = mm3(bb, (gth[:, half:], gtl[:, half:]))
        ys[0, pl.ds(2 * k, 2), :, half:] = right.reshape(2, rows, half)

    def p2_grad(k):
        aa = (pair(hi, 1, k), pair(lo, 1, k))
        a1 = (aa[0][:, half:], aa[1][:, half:])
        right = mm3(a1, (gh[half:, half:], gl[half:, half:]))
        ys[1, pl.ds(2 * k, 2), :, half:] = right.reshape(2, rows, half)
        left = mm3(aa, (gh[:, :half], gl[:, :half]))
        ys[1, pl.ds(2 * k, 2), :, :half] = left.reshape(2, rows, half)

    def p2_mix(b):
        bb = (hi[0, b], lo[0, b])
        aa = (hi[1, b], lo[1, b])
        b0 = (bb[0][:, :half], bb[1][:, :half])
        a0 = (aa[0][:, :half], aa[1][:, :half])
        a1 = (aa[0][:, half:], aa[1][:, half:])
        macc[:half, :half] += mm3(a0, b0, 0, 0)
        macc[half:, :] += mm3(a1, bb, 0, 0)

    def handle(w, k, i, sends, takes):
        b, c, part = x * GROUP + k, k * cuts + i, cut(i)
        first = x == w
        if sends:
            x_copy(w, c).wait_recv()
        else:
            @pl.when(jnp.logical_not(first))
            def _():
                x_copy(w, c).wait_recv()

        if takes:
            z_copy(w, c).wait_recv()

        own, other = pas[b, part][:, None, :], pasr[b, part][:, None, :]
        mine, theirs = loc[w, b, part], get(xr, w, c, piece)
        pass0, pass1 = jnp.where(first, own, other), jnp.where(first, other, own)
        loc0, loc1 = jnp.where(first, mine, theirs), jnp.where(first, theirs, mine)
        in0 = get(zr, w, c, piece) if takes else jnp.zeros_like(mine)
        in1 = pass0 * in0 + loc0
        if sends:
            put(zq, w, c, pass1 * in1 + loc1)
            z_copy(w, c).start()

        if takes:
            put(tq, w, c, jnp.where(first, in1, in0))
            t_copy(w, c).start()
        else:
            @pl.when(first)
            def _():
                put(tq, w, c, in1)
                t_copy(w, c).start()

        ins[w, b, part] = jnp.where(first, in0, in1)

    def grad(w, b, n):
        both = pairs[w, pl.ds(b, n)].reshape(n * rows, 2 * state)
        m = mm(both, hi[1 - w, pl.ds(b, n)].reshape(n * rows, tok), 0, 0)
        low = lo[1 - w, pl.ds(b, n)].reshape(n * rows, tok)
        gacc[w] += m[:state] + m[state:] + mm(both[:, :state], low, 0, 0)

    def ready(w, b):
        st = split((ins[w, b] * scl[1 - w, b][:, None, :]).reshape(rows, state))
        pairs[w, b] = jnp.concatenate(st, axis=1)

    def result(w, b):
        ready(w, b)
        y = ys[w, b] + mm(pairs[w, b], proj[1 - w], 1, 1)
        skip = skp[b][:, 0:1][:, :, None]
        res_ref[w, hblock(b)] = (
            y.reshape(hb, width, tok) * fac[1 - w, b][:, None, :]
            + skip * inp[w, hblock(b)].astype(F32)
        ).astype(BF16)

    def take(w, k):
        b = (1 - x) * GROUP + k

        def read():
            for i in range(cuts):
                t_copy(w, k * cuts + i).wait_recv()
                ins[w, b, cut(i)] = get(tr, w, k * cuts + i, piece)

        if w is late:
            read()
            return b

        none = edge & leads_early

        @pl.when(none)
        def _():
            ins[w, b] = jnp.zeros_like(ins[w, b])

        pl.when(jnp.logical_not(none))(read)
        return b

    def c_copy(w):
        return rcopy(gsc.at[w, 1 - core], grc.at[w], csem, (w,), me, mate)

    def y_copy(w, d, slot):
        return rcopy(hx.at[w, slot], hx.at[w, slot], ysem, (w, d), me, lax.rem(hd + 2 * d, nhead))

    def f_copy(w, slot):
        return rcopy(gfin.at[w, slot], gfin.at[w, slot], fsem, (w,), me, mate)

    def reduce_core(w):
        kept = seg_row == jnp.where(w == 0, prior, seg_last)
        g = gloc[w] + jnp.where(kept, gacc[w], 0.0)
        gsc[w, 0], gsc[w, 1] = g[:, :half], g[:, half:]
        c_copy(w).start()

    def reduce_rows(w):
        c_copy(w).wait_recv()
        v = gsc[w, core] + grc[w]
        top = jnp.max(jnp.abs(v), axis=0, keepdims=True)
        power = jnp.ceil(jnp.log2(jnp.maximum(top, 1e-30)))
        code = jnp.round(v * (jnp.exp2(-power) * 32000.0))
        hx[w, yy, :state] = code.astype(jnp.int32).astype(jnp.int16)
        hx[w, yy, state:] = (
            jnp.broadcast_to(power, (16, half)).astype(jnp.int32).astype(jnp.int16)
        )
        for d in range(1, ny):
            y_copy(w, d, yy).start()

    def reduce_end(w):
        for d in range(1, ny):
            y_copy(w, d, lax.rem(yy + ny - d, ny)).wait_recv()
        total = jnp.zeros((state, half), F32)
        for j in range(ny):
            power = hx[w, j, state:].astype(jnp.int32).astype(F32)[0:1]
            code = hx[w, j, :state].astype(jnp.int32).astype(F32)
            total = total + code * (jnp.exp2(power) * (1.0 / 32000.0))
        gfin[w, core] = total.T.astype(BF16)
        f_copy(w, core).start()

    @pl.loop(0, GROUP)
    def _(k):
        @pl.when(k == 0)
        def _():
            p_copy().wait_recv()

        @pl.when(edge)
        def _():
            handle(early, k, 0, True, False)

        p2_out(k)

    @pl.loop(0, GROUP)
    def _(k):
        @pl.when(jnp.logical_not(edge))
        def _():
            handle(early, k, 0, True, True)

        p2_grad(k)
        p2_mix(GROUP + k)

    @pl.loop(0, GROUP)
    def _(k):
        @pl.when(jnp.logical_not(edge))
        def _():
            for i in range(cuts):
                handle(late, k, i, True, True)

        result(early, x * GROUP + k)
        p2_mix(k)

    grad(early, x * GROUP, GROUP)
    mixed = split(jnp.where(same & (r_id >= c_id), macc[...], 0.0))
    keys, queries = key_ref[...], query_ref[...]
    gloc[0] = mm(keys, mixed[0], 0, 1) + mm(keys, mixed[1], 0, 1)
    gloc[1] = mm(queries, mixed[0], 0, 0) + mm(queries, mixed[1], 0, 0)

    @pl.loop(0, GROUP)
    def _(k):
        result(early, take(early, k))

    grad(early, (1 - x) * GROUP, GROUP)
    reduce_core(early)

    @pl.loop(0, GROUP)
    def _(k):
        @pl.when(edge)
        def _():
            for i in range(cuts):
                handle(late, k, i, False, True)

        result(late, x * GROUP + k)

        @pl.when(k == 1)
        def _():
            reduce_rows(early)

    grad(late, x * GROUP, GROUP)

    @pl.loop(0, GROUP)
    def _(k):
        b = take(late, k)
        result(late, b)
        grad(late, b, 1)

    reduce_core(late)
    reduce_rows(late)

    p_copy().wait_send()
    @pl.loop(0, GROUP * cuts)
    def _(k):
        x_copy(early, k).wait_send()
        z_copy(early, k).wait_send()
        t_copy(late, k).wait_send()

        @pl.when(jnp.logical_not(edge) | leads_late)
        def _():
            x_copy(late, k).wait_send()

        @pl.when(jnp.logical_not(edge) | leads_early)
        def _():
            t_copy(early, k).wait_send()

        @pl.when(jnp.logical_not(edge))
        def _():
            z_copy(late, k).wait_send()

    reduce_end(early)
    reduce_end(late)
    for w in range(2):
        f_copy(w, 1 - core).wait_recv()
    for j in range(2):
        gq_ref[j * half : (j + 1) * half] = gfin[0, j]
        gk_ref[j * half : (j + 1) * half] = gfin[1, j]

    for w in range(2):
        c_copy(w).wait_send()
        f_copy(w, core).wait_send()
        for d in range(1, ny):
            y_copy(w, d, yy).wait_send()


def store(res, gk, gq, out_ref, gs_ref, gk_ref, gq_ref, sems):
    pairs = ((res.at[0], out_ref), (res.at[1], gs_ref), (gk, gk_ref), (gq, gq_ref))
    copies = [pltpu.make_async_copy(a, b, sems.at[i]) for i, (a, b) in enumerate(pairs)]
    for copy in copies:
        copy.start()
    for copy in copies:
        copy.wait()


def solution(mesh):
    nseq, nhead = mesh.shape["seq"], mesh.shape["head"]

    def on_device(signal, step_raw, key_proj, query_proj, decay_log, skip_gain, lengths, cotangent):
        tok, heads, width = signal.shape
        state = key_proj.shape[1]
        blocks = 2 * GROUP
        hb = heads // blocks
        rows = hb * width
        half = tok // 2
        ny = nhead // 2
        dma = pltpu.SemaphoreType.DMA
        vmem = pltpu.VMEM
        cuts = 1
        chunks, hc = GROUP * cuts, hb // cuts
        st = (hb, width, state)
        scratch = (
            [pltpu.SMEM(lengths.shape, jnp.int32), vmem((heads, tok), BF16)]
            + [vmem((tok, state), BF16)] * 2
            + [vmem((1, heads), F32)] * 2
            + [vmem((2, heads, width, tok), BF16)]
            + [vmem((2, blocks, rows, tok), BF16)] * 2
            + [vmem((2, blocks, rows, tok), F32)]
            + [vmem((tok, tok), F32)]
            + [vmem((tok, tok), BF16)] * 4
            + [vmem((2, tok, 2 * state), BF16)]
            + [vmem((2, 2 * tok, state), BF16)]
            + [vmem((2, blocks, hb, tok), F32)]
            + [vmem((blocks, hb, state), F32)] * 2
            + [vmem((2, blocks, hb, state), F32)]
            + [vmem((blocks, hb, state), F32)]
            + [vmem((2, blocks) + st, F32)] * 2
            + [vmem((2, chunks, hc * width + 16, state), jnp.int16)] * 6
            + [vmem((2, blocks, rows, 2 * state), BF16)]
            + [vmem((2, state, tok), F32)] * 2
            + [vmem((2, 2, state, half), F32)]
            + [vmem((2, state, half), F32)]
            + [vmem((2, ny, state + 16, half), jnp.int16)]
            + [vmem((2, 2, half, state), BF16)]
            + [dma((6,)), dma((2, 2, 2)), dma((2,))]
            + [dma((2, 2, chunks))] * 3
            + [dma((2, 2)), dma((2, 2, ny)), dma((2, 2))]
        )
        turned = jax.ShapeDtypeStruct((heads, width, tok), BF16)
        grads = jax.ShapeDtypeStruct((tok, state), BF16)
        whole = pl.BlockSpec(memory_space=pltpu.VMEM)
        anywhere = pl.BlockSpec(memory_space=pl.ANY)
        res, gk, gq = pl.pallas_call(
            functools.partial(kernel, nseq, nhead),
            out_shape=(
                vmem((2, heads, width, tok), BF16), vmem((tok, state), BF16), vmem((tok, state), BF16)
            ),
            in_specs=[anywhere] * 8,
            out_specs=(whole,) * 3,
            scratch_shapes=scratch,
            compiler_params=pltpu.CompilerParams(
                collective_id=0, has_side_effects=True, vmem_limit_bytes=58 << 20
            ),
        )(
            lengths,
            jnp.transpose(signal, (1, 2, 0)),
            jnp.transpose(cotangent, (1, 2, 0)),
            step_raw.T,
            key_proj,
            query_proj,
            decay_log[None, :],
            skip_gain[None, :],
        )
        out, gs, gk, gq = pl.pallas_call(
            store,
            out_shape=(turned, turned, grads, grads),
            in_specs=[whole] * 3,
            out_specs=(anywhere,) * 4,
            scratch_shapes=[dma((4,))],
            compiler_params=pltpu.CompilerParams(vmem_limit_bytes=2 << 20),
        )(*(pltpu.with_memory_space_constraint(v, pltpu.VMEM) for v in (res, gk, gq)))
        return jnp.transpose(out, (2, 0, 1)), jnp.transpose(gs, (2, 0, 1)), gk, gq

    in_specs = (
        P("seq", "head", None),
        P("seq", "head"),
        P("seq", None),
        P("seq", None),
        P("head"),
        P("head"),
        P(),
        P("seq", "head", None),
    )
    out_specs = (P("seq", "head", None), P("seq", "head", None), P("seq", None), P("seq", None))
    return jax.shard_map(
        on_device, mesh=mesh, in_specs=in_specs, out_specs=out_specs, check_vma=False
    )
```
